32 devices in a mesh: dp: 4 (over y, core), fsdp: 8 (over z, x).
Axes of the slice: x: 2, y: 2, z: 4, core: 2. Of those that a mesh axis runs over, the one named last changes fastest.
Arguments:
- context: bfloat16 [16384, 1024], P(('dp', 'fsdp')), may hold values from -6 to 6
- residual: bfloat16 [16384, 2048], P(('dp', 'fsdp')), may hold values from -6 to 6
- out_weight: bfloat16 [1024, 2048], P('fsdp'), may hold values from -0.1875 to 0.1875
- norm_gain: float32 [2048], replicated, may hold values from 0.5 to 1.5
- user_vectors: bfloat16 [256, 2048], P(('dp', 'fsdp')), may hold values from -12 to 12
- positive: int32 [256], P(('dp', 'fsdp')), may hold values from 0 to 63
- item_ids: int32 [64], P(('dp', 'fsdp')), may hold values from 0 to 31
- item_counts: int32 [64], P(('dp', 'fsdp')), may hold values from 1 to 5000
- lengths: int32 [64], P(('dp', 'fsdp')), may hold values from 64 to 256
Outputs:
- mean_loss: float32 [], replicated
- residual_grad: bfloat16 [16384, 2048], P(('dp', 'fsdp'))
- context_grad: bfloat16 [16384, 1024], P(('dp', 'fsdp'))
- weight_grad: bfloat16 [1024, 2048], P('fsdp')
- norm_gain_grad: float32 [2048], replicated
- user_grad: bfloat16 [256, 2048], P(('dp', 'fsdp'))
The draws below stay inside these ranges and needn't reach their ends.
All inputs are finite; a program needn't handle non-finite values.
Results may differ from the reference program's by a relative error of at most 0.015.
Values may be sent and summed in bfloat16 or wider, within the bound.
A program may use at most 128 MiB of HBM per device.

```python
import math
import jax
import jax.numpy as jnp
import numpy as np
from jax import lax

D = 2048
H = 1024
LENGTH = 256
ITEMS = 64
USER_COUNT = 256
TOKENS = 16384


def draw_user_vectors(key, part):
    key_normal = jax.random.fold_in(key, 11)
    row_index = jnp.arange(USER_COUNT, dtype=jnp.float32)
    row_factor = 0.05 * (1.0 + 2.0 * row_index / max(USER_COUNT - 1, 1))
    normed_share = jax.random.normal(key_normal, (USER_COUNT, D), jnp.float32)
    value_rows = normed_share * row_factor[:, None]
    return jnp.clip(value_rows, -12.0, 12.0).astype(jnp.bfloat16)


def plant(entries, key, smallest, largest):
    longest = entries.shape.index(max(entries.shape))
    spots = []
    for shift in (0, 1):
        where = [jax.random.randint(jax.random.fold_in(key, axis), (), 0, length) for axis, length in enumerate(entries.shape)]
        where[longest] = (where[longest] + shift) % entries.shape[longest]
        spots.append(tuple(where))
    return entries.at[spots[0]].set(smallest).at[spots[1]].set(largest)


def shard_levels(stream_key, extent, split, low, high):
    loudness = 1.0
    for axis_at, blocks in split:
        draws = jax.random.uniform(jax.random.fold_in(jax.random.fold_in(stream_key, 6), axis_at), (blocks,), jnp.float32, low / len(split), high / len(split))
        loudness = loudness * jnp.repeat(jnp.exp(draws), extent[axis_at] // blocks).reshape((-1,) + (1,) * (len(extent) - 1 - axis_at))
    return loudness


def rank_table(count, slope):
    loads = [(1 << 20) // math.isqrt(rank ** slope) + 1 for rank in range(1, count + 1)]
    spread = 1 + sum(loads) // (1 << 30)
    return np.cumsum(np.array([max(1, weight // spread) for weight in loads]))


def ranked_ids(own_key, shape, number_of, skew):
    listing = rank_table(number_of, skew)
    pick = jax.random.randint(jax.random.fold_in(own_key, 1), shape, 0, int(listing[number_of - 1]))
    grade = jnp.searchsorted(jnp.asarray(listing, jnp.int32), pick, side="right")
    return jax.random.permutation(jax.random.fold_in(own_key, 2), number_of)[grade].astype(jnp.int32)


def gaussian(stream_key, dims, scale, limit, cuts=(), kind=jnp.bfloat16):
    entries = jax.random.normal(stream_key, dims, jnp.float32) * scale
    if len(cuts) > 0:
        entries = shard_levels(stream_key, dims, cuts, -0.22, 0.18) * entries
    return jnp.clip(entries, min=-limit, max=limit).astype(kind)


def setup_inputs(seed: int = 0) -> dict:
    splits = jax.random.split(jax.random.key(seed), 10)
    context = gaussian(splits[0], (TOKENS, H), 1.0, 6.0, ((0, 32),))
    residual = gaussian(splits[1], (TOKENS, D), 1.0, 6.0, ((0, 32),))
    out_weight = gaussian(splits[2], (H, D), H ** -0.5, 0.1875, ((0, 8),))
    norm_gain = jnp.clip(1.0 + 0.1 * jax.random.normal(splits[3], (D,), jnp.float32), 0.5, 1.5)
    user_vectors = draw_user_vectors(jax.random.fold_in(splits[9], 71), 0)
    positive = plant(jax.random.randint(splits[5], (USER_COUNT,), 0, ITEMS), jax.random.fold_in(splits[5], 1), 0, ITEMS - 1).astype(jnp.int32)
    item_ids = plant(ranked_ids(splits[6], (ITEMS,), ITEMS // 2, 2), jax.random.fold_in(splits[6], 3), 0, (ITEMS // 2) - 1).astype(jnp.int32)
    item_counts = plant(jax.random.randint(splits[7], (ITEMS,), 1, 5001), jax.random.fold_in(splits[7], 1), 1, 5000).astype(jnp.int32)
    lengths = plant(jax.random.randint(splits[8], (ITEMS,), LENGTH // 4, LENGTH + 1), jax.random.fold_in(splits[8], 1), LENGTH // 4, LENGTH).astype(jnp.int32)
    return dict(context=context, residual=residual, out_weight=out_weight, norm_gain=norm_gain, user_vectors=user_vectors, positive=positive, item_ids=item_ids, item_counts=item_counts, lengths=lengths)


EPSILON = 1e-06
MASKED_FILL = -1e+30

def stream_of(context_rows, residual_rows, out_weight, norm_gain):
    attended = jnp.dot(context_rows, out_weight, preferred_element_type=jnp.float32)
    stream = residual_rows.astype(jnp.float32) + attended
    inverse_root_mean = lax.rsqrt(lax.optimization_barrier(jnp.mean(stream * stream, axis=-1, keepdims=True)) + EPSILON)
    return (stream, inverse_root_mean, stream * inverse_root_mean * norm_gain)

def reference(context, residual, out_weight, norm_gain, user_vectors, positive, item_ids, item_counts, lengths):
    context_items = context.reshape(ITEMS, LENGTH, H)
    residual_items = residual.reshape(ITEMS, LENGTH, D)
    positions = jnp.arange(LENGTH, dtype=jnp.int32)

    def pool_item(packed):
        context_rows, residual_rows, length_here = packed
        stream, inverse_root_mean, normed = stream_of(context_rows, residual_rows, out_weight, norm_gain)
        inside = (positions < length_here)[:, None]
        return lax.optimization_barrier(jnp.sum(jnp.where(inside, normed, 0.0), axis=0)) / length_here.astype(jnp.float32)
    pooled = lax.map(pool_item, (context_items, residual_items, lengths))
    emb_scale = lax.rsqrt(lax.optimization_barrier(jnp.mean(pooled * pooled, axis=-1, keepdims=True)) + EPSILON)
    embedding = (pooled * emb_scale).astype(jnp.bfloat16)
    scores = jnp.dot(user_vectors, embedding.T, preferred_element_type=jnp.float32)
    columns = jnp.arange(ITEMS, dtype=jnp.int32)
    onehot = columns[None, :] == positive[:, None]
    positive_id = lax.optimization_barrier(jnp.sum(jnp.where(onehot, item_ids[None, :], 0), axis=1))
    excluded = (item_ids[None, :] == positive_id[:, None]) & jnp.logical_not(onehot)
    log_counts = jnp.log(item_counts.astype(jnp.float32))
    logits = jnp.where(excluded, MASKED_FILL, scores - log_counts[None, :])
    row_max = lax.optimization_barrier(jnp.max(logits, axis=1, keepdims=True))
    weights = jnp.where(excluded, 0.0, jnp.exp(logits - row_max))
    row_total = lax.optimization_barrier(jnp.sum(weights, axis=1, keepdims=True))
    log_total = row_max[:, 0] + jnp.log(row_total[:, 0])
    picked = lax.optimization_barrier(jnp.sum(jnp.where(onehot, logits, 0.0), axis=1))
    mean_loss = jnp.mean(log_total - picked)
    logit_grad = (weights / row_total - onehot.astype(jnp.float32)).astype(jnp.bfloat16)
    user_grad = jnp.dot(logit_grad, embedding, preferred_element_type=jnp.float32).astype(jnp.bfloat16)
    emb_grad = jnp.dot(logit_grad.T, user_vectors, preferred_element_type=jnp.float32)
    pooled_grad = emb_scale * emb_grad - pooled * emb_scale ** 3 * lax.optimization_barrier(jnp.mean(pooled * emb_grad, axis=-1, keepdims=True))

    def backward_item(carried, packed):
        weight_sum, gain_sum = carried
        context_rows, residual_rows, length_here, grad_row = packed
        stream, inverse_root_mean, normed = stream_of(context_rows, residual_rows, out_weight, norm_gain)
        inside = (positions < length_here)[:, None]
        normed_grad = jnp.where(inside, grad_row[None, :] / length_here.astype(jnp.float32), 0.0)
        gain_sum = gain_sum + lax.optimization_barrier(jnp.sum(normed_grad * stream * inverse_root_mean, axis=0))
        scaled = norm_gain * normed_grad
        stream_grad = inverse_root_mean * scaled - stream * inverse_root_mean ** 3 * lax.optimization_barrier(jnp.mean(scaled * stream, axis=-1, keepdims=True))
        residual_grad = stream_grad.astype(jnp.bfloat16)
        context_grad = jnp.dot(residual_grad, out_weight.T, preferred_element_type=jnp.float32).astype(jnp.bfloat16)
        weight_sum = weight_sum + jnp.dot(context_rows.T, residual_grad, preferred_element_type=jnp.float32)
        return ((weight_sum, gain_sum), (residual_grad, context_grad))
    start_sums = (jnp.zeros((H, D), jnp.float32), jnp.zeros((D,), jnp.float32))
    final_sums, outputs = lax.scan(backward_item, start_sums, (context_items, residual_items, lengths, pooled_grad))
    weight_sum, gain_sum = final_sums
    residual_grad = outputs[0].reshape(TOKENS, D)
    context_grad = outputs[1].reshape(TOKENS, H)
    return (mean_loss, residual_grad, context_grad, weight_sum.astype(jnp.bfloat16), gain_sum, user_grad)
```

```python
import functools

import jax
import jax.numpy as jnp
from jax import lax
from jax.experimental import pallas as pl
from jax.experimental.pallas import tpu as pltpu
from jax.sharding import PartitionSpec as P

EPSILON = 1e-06
MASKED_FILL = -1e30
MESH = pl.DeviceIdType.MESH
CHUNKS = 4


def contract_rows(left, right):
    return lax.dot_general(
        left, right, (((0,), (0,)), ((), ())), preferred_element_type=jnp.float32
    )


def contract_last(left, right):
    return lax.dot_general(
        left, right, (((1,), (1,)), ((), ())), preferred_element_type=jnp.float32
    )


def ring_place(index, count):
    return jnp.where(index % 2 == 0, index // 2, count - 1 - index // 2)


def ring_index(place, count):
    return jnp.where(place < count // 2, 2 * place, 2 * (count - 1 - place) + 1)


def greet(devices):
    barrier = pltpu.get_barrier_semaphore()
    for device in devices:
        pl.semaphore_signal(barrier, inc=1, device_id=device, device_id_type=MESH)
    pl.semaphore_wait(barrier, len(devices))


def greet_all(groups, ring, me):
    total = groups * ring
    barrier = pltpu.get_barrier_semaphore()

    def signal(k, carry):
        peer = lax.rem(me + k, total)
        pl.semaphore_signal(
            barrier, inc=1, device_id=(peer // ring, lax.rem(peer, ring)), device_id_type=MESH
        )
        return carry

    lax.fori_loop(1, total, signal, 0)
    pl.semaphore_wait(barrier, total - 1)


def remote(src, dst, send_sem, recv_sem, device):
    return pltpu.make_async_remote_copy(
        src_ref=src,
        dst_ref=dst,
        send_sem=send_sem,
        recv_sem=recv_sem,
        device_id=device,
        device_id_type=MESH,
    )


def gather_kernel(
    groups, ring, w_in, u_in, k_in, w_out, u_out, k_out,
    own_sem, w_send, w_recv, p_send, p_recv, u_send, u_recv, k_send, k_recv,
    du_send, du_recv, dk_send, dk_recv,
):
    group, index = lax.axis_index("dp"), lax.axis_index("fsdp")
    core = lax.rem(group, 2)
    partner = group + 1 - 2 * core
    step = 1 - 2 * core
    place = ring_place(index, ring)
    rows = w_in.shape[0]
    half = rows // 2
    part = half // CHUNKS
    following = ring_index(lax.rem(place + ring + step, ring), ring)
    previous = ring_index(lax.rem(place + ring - step, ring), ring)

    def owner(s, way=step):
        return ring_index(lax.rem(place + ring * ring - s * way, ring), ring)

    def w_slice(who, c, side=core):
        start = pl.multiple_of(who * rows + side * half + c * part, part)
        return w_out.at[pl.ds(start, part), :]

    greet(
        [(lax.rem(group + k, groups), index) for k in range(1, groups)]
        + [(group, following), (group, previous)]
    )
    own = [
        pltpu.make_async_copy(
            w_in, w_out.at[pl.ds(pl.multiple_of(index * rows, rows), rows), :], own_sem.at[0]
        ),
        pltpu.make_async_copy(u_in, u_out.at[group * ring + index], own_sem.at[1]),
        pltpu.make_async_copy(k_in, k_out.at[group * ring + index], own_sem.at[2]),
    ]
    for copy in own:
        copy.start()
    for copy in own:
        copy.wait()

    def w_ring(s, c):
        ref = w_slice(owner(s), c)
        return remote(ref, ref, w_send.at[s, c], w_recv.at[s, c], (group, following))

    def w_ring_in(s, c):
        ref = w_slice(owner(s + 1), c)
        return remote(ref, ref, w_send.at[s, c], w_recv.at[s, c], (group, following))

    def w_part(s, c):
        ref = w_slice(owner(s + 1), c)
        return remote(ref, ref, p_send.at[s, c], p_recv.at[s, c], (partner, index))

    def w_part_in(s, c):
        ref = w_slice(owner(s + 1, -step), c, 1 - core)
        return remote(ref, ref, p_send.at[s, c], p_recv.at[s, c], (partner, index))

    small = ((u_out, u_send, u_recv, du_send, du_recv), (k_out, k_send, k_recv, dk_send, dk_recv))

    def s_ring(a, s, shift):
        out, send, recv, _, _ = small[a]
        ref = out.at[group * ring + owner(s + shift)]
        return remote(ref, ref, send.at[s], recv.at[s], (group, following))

    def s_out(a, s, k):
        out, _, _, send, recv = small[a]
        ref = out.at[group * ring + owner(s)]
        peer = lax.rem(group + k, groups)
        return remote(ref, ref, send.at[s, k - 1], recv.at[s, k - 1], (peer, index))

    def s_in(a, s, k):
        out, _, _, send, recv = small[a]
        source = lax.rem(group + groups - k, groups)
        way = 1 - 2 * lax.rem(source, 2)
        ref = out.at[source * ring + owner(s, way)]
        return remote(ref, ref, send.at[s, k - 1], recv.at[s, k - 1], (source, index))

    for c in range(CHUNKS):
        w_ring(0, c).start()
    for a in (0, 1):
        s_ring(a, 0, 0).start()
        for k in range(1, groups):
            s_out(a, 0, k).start()

    def forward(s, carry):
        for c in range(CHUNKS):
            w_ring_in(s - 1, c).wait_recv()
            w_ring(s, c).start()
            w_part(s - 1, c).start()
        for a in (0, 1):
            s_ring(a, s - 1, 1).wait_recv()
            s_ring(a, s, 0).start()
            for k in range(1, groups):
                s_out(a, s, k).start()
        return carry

    lax.fori_loop(1, ring - 1, forward, 0)
    last = ring - 1
    for c in range(CHUNKS):
        w_ring_in(last - 1, c).wait_recv()
        w_part(last - 1, c).start()
    for a in (0, 1):
        s_ring(a, last - 1, 1).wait_recv()
        for k in range(1, groups):
            s_out(a, last, k).start()

    def finish(s, carry):
        for c in range(CHUNKS):
            w_ring(s, c).wait_send()
            w_part(s, c).wait_send()
            w_part_in(s, c).wait_recv()
        for a in (0, 1):
            s_ring(a, s, 0).wait_send()
        return carry

    lax.fori_loop(0, ring - 1, finish, 0)

    def finish_small(s, carry):
        for a in (0, 1):
            for k in range(1, groups):
                s_out(a, s, k).wait_send()
                s_in(a, s, k).wait_recv()
        return carry

    lax.fori_loop(0, ring, finish_small, 0)


def gather_inputs(groups, ring, weight, users, keys):
    total = groups * ring
    rows, width = weight.shape
    dma = pltpu.SemaphoreType.DMA
    vmem = pl.BlockSpec(memory_space=pltpu.VMEM)
    anywhere = pl.BlockSpec(memory_space=pl.ANY)
    return pl.pallas_call(
        functools.partial(gather_kernel, groups, ring),
        out_shape=(
            jax.ShapeDtypeStruct((ring * rows, width), weight.dtype),
            jax.ShapeDtypeStruct((total,) + users.shape, users.dtype),
            jax.ShapeDtypeStruct((total,) + keys.shape, keys.dtype),
        ),
        in_specs=[anywhere, anywhere, anywhere],
        out_specs=(vmem, vmem, vmem),
        scratch_shapes=[dma((3,))]
        + [dma((ring - 1, CHUNKS))] * 4
        + [dma((ring - 1,))] * 4
        + [dma((ring, groups - 1))] * 4,
        compiler_params=pltpu.CompilerParams(
            collective_id=0, has_side_effects=True, vmem_limit_bytes=32 << 20
        ),
        name="gather_inputs",
    )(weight, users, keys)


def share_kernel(groups, ring, x_in, x_out, own_sem, send_sem, recv_sem):
    total = groups * ring
    me = lax.axis_index("dp") * ring + lax.axis_index("fsdp")
    greet_all(groups, ring, me)

    def push(k):
        peer = lax.rem(me + k, total)
        return remote(
            x_in, x_out.at[me], send_sem.at[k - 1], recv_sem.at[k - 1],
            (peer // ring, lax.rem(peer, ring)),
        )

    def pull(k):
        source = lax.rem(me + total - k, total)
        return remote(
            x_in, x_out.at[source], send_sem.at[k - 1], recv_sem.at[k - 1],
            (source // ring, lax.rem(source, ring)),
        )

    def start(k, carry):
        push(k).start()
        return carry

    def finish(k, carry):
        push(k).wait_send()
        pull(k).wait_recv()
        return carry

    lax.fori_loop(1, total, start, 0)
    own = pltpu.make_async_copy(x_in, x_out.at[me], own_sem)
    own.start()
    own.wait()
    lax.fori_loop(1, total, finish, 0)


def share(groups, ring, block):
    total = groups * ring
    dma = pltpu.SemaphoreType.DMA
    vmem = pl.BlockSpec(memory_space=pltpu.VMEM)
    return pl.pallas_call(
        functools.partial(share_kernel, groups, ring),
        out_shape=jax.ShapeDtypeStruct((total,) + block.shape, block.dtype),
        in_specs=[vmem],
        out_specs=vmem,
        scratch_shapes=[dma, dma((total - 1,)), dma((total - 1,))],
        compiler_params=pltpu.CompilerParams(collective_id=1, has_side_effects=True),
        name="share",
    )(block)


def reduce_kernel(
    groups, ring, part_in, gain_in, out, gain_out,
    cross, held, arrived, totals,
    own_sem, g_send, g_recv, x_send, x_recv, r_send, r_recv, t_send, t_recv, o_send, o_recv,
):
    total = groups * ring
    group, index = lax.axis_index("dp"), lax.axis_index("fsdp")
    me = group * ring + index
    core = lax.rem(group, 2)
    partner = group + 1 - 2 * core
    step = 1 - 2 * core
    place = ring_place(index, ring)
    rows = part_in.shape[0] // ring
    half = rows // 2
    piece = half // CHUNKS
    lines = groups // 2
    line = group // 2
    following = ring_index(lax.rem(place + ring + step, ring), ring)

    def owner(s, way=step):
        return ring_index(lax.rem(place + ring * ring - (s + 1) * way, ring), ring)

    greet_all(groups, ring, me)

    def cross_out(s):
        who = owner(s, -step)
        start = pl.multiple_of(who * rows + (1 - core) * half, half)
        return remote(
            part_in.at[pl.ds(start, half), :], cross.at[s], x_send.at[s], x_recv.at[s],
            (partner, index),
        )

    def start_cross(s, carry):
        cross_out(s).start()
        return carry

    lax.fori_loop(0, ring, start_cross, 0)

    def gain_push(k):
        peer = lax.rem(me + k, total)
        return remote(
            gain_in, gain_out.at[me], g_send.at[k - 1], g_recv.at[k - 1],
            (peer // ring, lax.rem(peer, ring)),
        )

    def gain_pull(k):
        source = lax.rem(me + total - k, total)
        return remote(
            gain_in, gain_out.at[source], g_send.at[k - 1], g_recv.at[k - 1],
            (source // ring, lax.rem(source, ring)),
        )

    def start_gain(k, carry):
        gain_push(k).start()
        return carry

    lax.fori_loop(1, total, start_gain, 0)
    own = pltpu.make_async_copy(gain_in, gain_out.at[me], own_sem)
    own.start()

    def ring_copy(s, c):
        at = pl.ds(c * piece, piece)
        return remote(
            held.at[s, at, :], arrived.at[s, at, :], r_send.at[s, c], r_recv.at[s, c],
            (group, following),
        )

    def local_term(s, c):
        start = pl.multiple_of(owner(s) * rows + core * half + c * piece, piece)
        mine = part_in[pl.ds(start, piece), :].astype(jnp.float32)
        return mine + cross[s, pl.ds(c * piece, piece), :].astype(jnp.float32)

    cross_out(0).wait_recv()
    for c in range(CHUNKS):
        held[0, pl.ds(c * piece, piece), :] = local_term(0, c).astype(held.dtype)
        ring_copy(0, c).start()

    def pass_on(s, carry):
        cross_out(s).wait_recv()
        for c in range(CHUNKS):
            at = pl.ds(c * piece, piece)
            term = local_term(s, c)
            ring_copy(s - 1, c).wait_recv()
            held[s, at, :] = (term + arrived[s - 1, at, :].astype(jnp.float32)).astype(held.dtype)
            ring_copy(s, c).start()
        return carry

    lax.fori_loop(1, ring - 1, pass_on, 0)
    last = ring - 1
    cross_out(last).wait_recv()

    def total_copy(k, c):
        at = pl.ds(c * piece, piece)
        ref = totals.at[line, at, :]
        return remote(
            ref, ref, t_send.at[k - 1, c], t_recv.at[k - 1, c],
            (lax.rem(group + 2 * k, groups), index),
        )

    def total_in(k, c):
        at = pl.ds(c * piece, piece)
        source = lax.rem(group + groups - 2 * k, groups)
        ref = totals.at[source // 2, at, :]
        return remote(ref, ref, t_send.at[k - 1, c], t_recv.at[k - 1, c], (source, index))

    for c in range(CHUNKS):
        at = pl.ds(c * piece, piece)
        term = local_term(last, c)
        ring_copy(last - 1, c).wait_recv()
        totals[line, at, :] = (term + arrived[last - 1, at, :].astype(jnp.float32)).astype(
            totals.dtype
        )
        for k in range(1, lines):
            total_copy(k, c).start()

    def out_copy(c, side):
        ref = out.at[pl.ds(pl.multiple_of(side * half + c * piece, piece), piece), :]
        return remote(ref, ref, o_send.at[c], o_recv.at[c], (partner, index))

    for c in range(CHUNKS):
        at = pl.ds(c * piece, piece)
        for k in range(1, lines):
            total_in(k, c).wait_recv()
        value = totals[0, at, :].astype(jnp.float32)
        for j in range(1, lines):
            value = value + totals[j, at, :].astype(jnp.float32)
        out[pl.ds(pl.multiple_of(core * half + c * piece, piece), piece), :] = value.astype(
            out.dtype
        )
        out_copy(c, core).start()

    def finish_cross(s, carry):
        cross_out(s).wait_send()
        return carry

    lax.fori_loop(0, ring, finish_cross, 0)

    def finish_ring(s, carry):
        for c in range(CHUNKS):
            ring_copy(s, c).wait_send()
        return carry

    lax.fori_loop(0, ring - 1, finish_ring, 0)
    own.wait()

    def finish_gain(k, carry):
        gain_push(k).wait_send()
        gain_pull(k).wait_recv()
        return carry

    lax.fori_loop(1, total, finish_gain, 0)
    for c in range(CHUNKS):
        for k in range(1, lines):
            total_copy(k, c).wait_send()
        out_copy(c, core).wait_send()
        out_copy(c, 1 - core).wait_recv()


def reduce_weight(groups, ring, partial, gain):
    total = groups * ring
    rows = partial.shape[0] // ring
    half, width = rows // 2, partial.shape[1]
    dma = pltpu.SemaphoreType.DMA
    vmem = pl.BlockSpec(memory_space=pltpu.VMEM)
    return pl.pallas_call(
        functools.partial(reduce_kernel, groups, ring),
        out_shape=(
            jax.ShapeDtypeStruct((rows, width), partial.dtype),
            jax.ShapeDtypeStruct((total,) + gain.shape, gain.dtype),
        ),
        in_specs=[vmem, vmem],
        out_specs=(vmem, vmem),
        scratch_shapes=[
            pltpu.VMEM((ring, half, width), partial.dtype),
            pltpu.VMEM((ring - 1, half, width), partial.dtype),
            pltpu.VMEM((ring - 1, half, width), partial.dtype),
            pltpu.VMEM((groups // 2, half, width), partial.dtype),
            dma,
            dma((total - 1,)),
            dma((total - 1,)),
            dma((ring,)),
            dma((ring,)),
            dma((ring - 1, CHUNKS)),
            dma((ring - 1, CHUNKS)),
            dma((groups // 2 - 1, CHUNKS)),
            dma((groups // 2 - 1, CHUNKS)),
            dma((CHUNKS,)),
            dma((CHUNKS,)),
        ],
        compiler_params=pltpu.CompilerParams(
            collective_id=2, has_side_effects=True, vmem_limit_bytes=40 << 20
        ),
        name="reduce_weight",
    )(partial, gain)


def on_device(
    groups, ring,
    context, residual, out_weight, norm_gain, user_vectors, positive, item_ids, item_counts, lengths
):
    tok_rows, head_width = context.shape
    model_width = residual.shape[1]
    items_here = lengths.shape[0]
    item_length = tok_rows // items_here
    users_here = user_vectors.shape[0]
    devices_all = groups * ring
    lanes = 128 * pl.cdiv(max(users_here, items_here), 128)
    keys = jnp.stack(
        [jnp.pad(row, (0, lanes - row.shape[0])) for row in (positive, item_ids, item_counts)]
    )
    keys = jnp.pad(keys, ((0, 5), (0, 0)))
    weight_all, users_all, keys_all = gather_inputs(groups, ring, out_weight, user_vectors, keys)
    users_all = users_all.reshape(devices_all * users_here, model_width)
    positive_all = keys_all[:, 0, :users_here].reshape(-1)
    ids_all = keys_all[:, 1, :items_here].reshape(-1)
    counts_all = keys_all[:, 2, :items_here].reshape(-1)
    attended = jnp.dot(context, weight_all, preferred_element_type=jnp.float32)
    stream = residual.astype(jnp.float32) + attended
    inverse_root_mean = lax.rsqrt(jnp.mean(stream * stream, axis=-1, keepdims=True) + EPSILON)
    normed = stream * inverse_root_mean * norm_gain
    positions = jnp.arange(item_length, dtype=jnp.int32)
    inside = (positions[None, :] < lengths[:, None])[:, :, None]
    length_float = lengths.astype(jnp.float32)[:, None]
    normed_items = normed.reshape(items_here, item_length, model_width)
    pooled = jnp.sum(jnp.where(inside, normed_items, 0.0), axis=1) / length_float
    emb_scale = lax.rsqrt(jnp.mean(pooled * pooled, axis=-1, keepdims=True) + EPSILON)
    embedding = (pooled * emb_scale).astype(jnp.bfloat16)
    emb_all = share(groups, ring, embedding).reshape(devices_all * items_here, model_width)
    me = lax.axis_index("dp") * ring + lax.axis_index("fsdp")
    items_all = jnp.arange(ids_all.shape[0], dtype=jnp.int32)
    onehot = items_all[None, :] == positive_all[:, None]
    positive_id = jnp.sum(jnp.where(onehot, ids_all[None, :], 0), axis=1)
    excluded = (ids_all[None, :] == positive_id[:, None]) & jnp.logical_not(onehot)
    scores = contract_last(users_all, emb_all)
    log_counts = jnp.log(counts_all.astype(jnp.float32))
    logits = jnp.where(excluded, MASKED_FILL, scores - log_counts[None, :])
    row_max = jnp.max(logits, axis=1, keepdims=True)
    weights = jnp.where(excluded, 0.0, jnp.exp(logits - row_max))
    row_total = jnp.sum(weights, axis=1, keepdims=True)
    log_total = row_max[:, 0] + jnp.log(row_total[:, 0])
    mean_loss = jnp.mean(log_total - jnp.sum(jnp.where(onehot, logits, 0.0), axis=1))
    logit_grad = (weights / row_total - onehot.astype(jnp.float32)).astype(jnp.bfloat16)
    own_users = lax.dynamic_slice_in_dim(logit_grad, me * users_here, users_here, axis=0)
    user_grad = jnp.dot(own_users, emb_all, preferred_element_type=jnp.float32).astype(
        jnp.bfloat16
    )
    own_items = lax.dynamic_slice_in_dim(logit_grad, me * items_here, items_here, axis=1)
    emb_grad = contract_rows(own_items, users_all)
    pooled_grad = emb_scale * emb_grad - pooled * emb_scale**3 * jnp.mean(
        pooled * emb_grad, axis=-1, keepdims=True
    )
    normed_grad = jnp.where(inside, pooled_grad[:, None, :] / length_float[:, :, None], 0.0)
    normed_grad = normed_grad.reshape(tok_rows, model_width)
    gain_part = jnp.sum(normed_grad * stream * inverse_root_mean, axis=0)
    scaled = norm_gain * normed_grad
    stream_grad = inverse_root_mean * scaled - stream * inverse_root_mean**3 * jnp.mean(
        scaled * stream, axis=-1, keepdims=True
    )
    residual_grad = stream_grad.astype(jnp.bfloat16)
    context_grad = contract_last(residual_grad, weight_all).astype(jnp.bfloat16)
    partial = contract_rows(context, residual_grad).astype(jnp.bfloat16)
    weight_grad, gain_all = reduce_weight(groups, ring, partial, gain_part[None, :])
    gain_grad = jnp.sum(gain_all[:, 0, :], axis=0)
    return (mean_loss, residual_grad, context_grad, weight_grad, gain_grad, user_grad)


def solution(mesh):
    placed = (
        P(("dp", "fsdp"), None),
        P(("dp", "fsdp"), None),
        P("fsdp", None),
        P(),
        P(("dp", "fsdp"), None),
        P(("dp", "fsdp")),
        P(("dp", "fsdp")),
        P(("dp", "fsdp")),
        P(("dp", "fsdp")),
    )
    return jax.shard_map(
        functools.partial(on_device, mesh.shape["dp"], mesh.shape["fsdp"]),
        mesh=mesh,
        in_specs=placed,
        out_specs=(
            P(),
            P(("dp", "fsdp"), None),
            P(("dp", "fsdp"), None),
            P("fsdp", None),
            P(),
            P(("dp", "fsdp"), None),
        ),
        check_vma=False,
    )
```

```python
import functools

import jax
import jax.numpy as jnp
from jax import lax
from jax.experimental import pallas as pl
from jax.experimental.pallas import tpu as pltpu
from jax.sharding import PartitionSpec as P

EPSILON = 1e-06
MASKED_FILL = -1e30
MESH = pl.DeviceIdType.MESH
CHUNKS = 4


def contract_rows(left, right):
    return lax.dot_general(
        left, right, (((0,), (0,)), ((), ())), preferred_element_type=jnp.float32
    )


def contract_last(left, right):
    return lax.dot_general(
        left, right, (((1,), (1,)), ((), ())), preferred_element_type=jnp.float32
    )


def ring_place(index, count):
    return jnp.where(index % 2 == 0, index // 2, count - 1 - index // 2)


def ring_index(place, count):
    return jnp.where(place < count // 2, 2 * place, 2 * (count - 1 - place) + 1)


def greet(devices):
    barrier = pltpu.get_barrier_semaphore()
    for device in devices:
        pl.semaphore_signal(barrier, inc=1, device_id=device, device_id_type=MESH)
    pl.semaphore_wait(barrier, len(devices))


def greet_all(groups, ring, me):
    total = groups * ring
    barrier = pltpu.get_barrier_semaphore()

    def signal(k, carry):
        peer = lax.rem(me + k, total)
        pl.semaphore_signal(
            barrier, inc=1, device_id=(peer // ring, lax.rem(peer, ring)), device_id_type=MESH
        )
        return carry

    lax.fori_loop(1, total, signal, 0)
    pl.semaphore_wait(barrier, total - 1)


def remote(src, dst, send_sem, recv_sem, device):
    return pltpu.make_async_remote_copy(
        src_ref=src,
        dst_ref=dst,
        send_sem=send_sem,
        recv_sem=recv_sem,
        device_id=device,
        device_id_type=MESH,
    )


def gather_kernel(
    groups, ring, w_in, u_in, k_in, w_out, u_out, k_out,
    own_sem, w_send, w_recv, p_send, p_recv, y_send, y_recv,
    u_send, u_recv, k_send, k_recv, ul_send, ul_recv, kl_send, kl_recv,
    up_send, up_recv, kp_send, kp_recv,
):
    group, index = lax.axis_index("dp"), lax.axis_index("fsdp")
    lines = groups // 2
    split = lines == 2
    slots = CHUNKS - 1 if split else CHUNKS
    line = group // 2
    core = lax.rem(group, 2)
    partner = group + 1 - 2 * core
    across = lax.rem(group + 2, groups)
    step = 1 - 2 * core
    place = ring_place(index, ring)
    rows = w_in.shape[0]
    half = rows // 2
    part = half // CHUNKS
    following = ring_index(lax.rem(place + ring + step, ring), ring)
    previous = ring_index(lax.rem(place + ring - step, ring), ring)

    def owner(s, way=step):
        return ring_index(lax.rem(place + ring * ring - s * way, ring), ring)

    def chunk(j):
        if not split or j < CHUNKS - 2:
            return j
        return CHUNKS - 2 + (line if j == CHUNKS - 2 else 1 - line)

    def w_slice(who, j, side=core):
        start = pl.multiple_of(who * rows + side * half + chunk(j) * part, part)
        return w_out.at[pl.ds(start, part), :]

    greet(
        [(lax.rem(group + k, groups), index) for k in range(1, groups)]
        + [(group, following), (group, previous)]
    )
    own = [
        pltpu.make_async_copy(
            w_in, w_out.at[pl.ds(pl.multiple_of(index * rows, rows), rows), :], own_sem.at[0]
        ),
        pltpu.make_async_copy(u_in, u_out.at[group * ring + index], own_sem.at[1]),
        pltpu.make_async_copy(k_in, k_out.at[group * ring + index], own_sem.at[2]),
    ]
    for copy in own:
        copy.start()
    for copy in own:
        copy.wait()

    def w_ring(s, j, shift=0):
        ref = w_slice(owner(s + shift), j)
        return remote(ref, ref, w_send.at[s, j], w_recv.at[s, j], (group, following))

    def w_part(s, j):
        ref = w_slice(owner(s + 1), j)
        return remote(ref, ref, p_send.at[s, j], p_recv.at[s, j], (partner, index))

    def w_part_in(s, j):
        ref = w_slice(owner(s + 1, -step), j, 1 - core)
        return remote(ref, ref, p_send.at[s, j], p_recv.at[s, j], (partner, index))

    def w_across(s, j):
        ref = w_slice(owner(s + 1), j)
        return remote(ref, ref, y_send.at[s], y_recv.at[s], (across, index))

    small = (
        (u_out, u_send, u_recv, ul_send, ul_recv, up_send, up_recv),
        (k_out, k_send, k_recv, kl_send, kl_recv, kp_send, kp_recv),
    )

    def s_ring(a, s, shift):
        out, send, recv = small[a][:3]
        ref = out.at[group * ring + owner(s + shift)]
        return remote(ref, ref, send.at[s], recv.at[s], (group, following))

    def s_line(a, s, k):
        out, _, _, send, recv = small[a][:5]
        ref = out.at[group * ring + owner(s)]
        peer = lax.rem(group + 2 * k, groups)
        return remote(ref, ref, send.at[s, k - 1], recv.at[s, k - 1], (peer, index))

    def s_line_in(a, s, k):
        out, _, _, send, recv = small[a][:5]
        source = lax.rem(group + groups - 2 * k, groups)
        ref = out.at[source * ring + owner(s)]
        return remote(ref, ref, send.at[s, k - 1], recv.at[s, k - 1], (source, index))

    def s_part(a, s, k):
        out, send, recv = small[a][0], small[a][5], small[a][6]
        source = lax.rem(group + groups - 2 * k, groups)
        ref = out.at[source * ring + owner(s)]
        return remote(ref, ref, send.at[s, k], recv.at[s, k], (partner, index))

    def s_part_in(a, s, k):
        out, send, recv = small[a][0], small[a][5], small[a][6]
        source = lax.rem(partner + groups - 2 * k, groups)
        ref = out.at[source * ring + owner(s, -step)]
        return remote(ref, ref, send.at[s, k], recv.at[s, k], (partner, index))

    def w_pass(s):
        if split:
            w_across(s, CHUNKS - 1).wait_recv()
            w_part(s, CHUNKS - 1).start()

    def spread(s):
        for a in (0, 1):
            for k in range(1, lines):
                s_line(a, s, k).start()
            s_part(a, s, 0).start()

    def s_pass(s):
        for a in (0, 1):
            for k in range(1, lines):
                s_line_in(a, s, k).wait_recv()
                s_part(a, s, k).start()

    def receive(s, more):
        for j in range(slots):
            w_ring(s - 1, j, 1).wait_recv()
            if more:
                w_ring(s, j).start()
            if split and j == CHUNKS - 2:
                w_across(s - 1, j).start()
            w_part(s - 1, j).start()
        for a in (0, 1):
            s_ring(a, s - 1, 1).wait_recv()
            if more:
                s_ring(a, s, 0).start()
        spread(s)

    for j in range(slots):
        w_ring(0, j).start()
    for a in (0, 1):
        s_ring(a, 0, 0).start()
    spread(0)
    receive(1, True)
    s_pass(0)

    def forward(s, carry):
        receive(s, True)
        w_pass(s - 2)
        s_pass(s - 1)
        return carry

    lax.fori_loop(2, ring - 1, forward, 0)
    last = ring - 1
    receive(last, False)
    w_pass(last - 2)
    s_pass(last - 1)
    w_pass(last - 1)
    s_pass(last)

    def finish(s, carry):
        for j in range(slots):
            w_ring(s, j).wait_send()
        if split:
            w_across(s, CHUNKS - 2).wait_send()
        for j in range(CHUNKS):
            w_part(s, j).wait_send()
            w_part_in(s, j).wait_recv()
        for a in (0, 1):
            s_ring(a, s, 0).wait_send()
        return carry

    lax.fori_loop(0, ring - 1, finish, 0)

    def finish_small(s, carry):
        for a in (0, 1):
            for k in range(1, lines):
                s_line(a, s, k).wait_send()
            for k in range(lines):
                s_part(a, s, k).wait_send()
                s_part_in(a, s, k).wait_recv()
        return carry

    lax.fori_loop(0, ring, finish_small, 0)


def gather_inputs(groups, ring, weight, users, keys):
    total = groups * ring
    lines = groups // 2
    rows, width = weight.shape
    dma = pltpu.SemaphoreType.DMA
    vmem = pl.BlockSpec(memory_space=pltpu.VMEM)
    anywhere = pl.BlockSpec(memory_space=pl.ANY)
    return pl.pallas_call(
        functools.partial(gather_kernel, groups, ring),
        out_shape=(
            jax.ShapeDtypeStruct((ring * rows, width), weight.dtype),
            jax.ShapeDtypeStruct((total,) + users.shape, users.dtype),
            jax.ShapeDtypeStruct((total,) + keys.shape, keys.dtype),
        ),
        in_specs=[anywhere, anywhere, anywhere],
        out_specs=(vmem, vmem, vmem),
        scratch_shapes=[dma((3,))]
        + [dma((ring - 1, CHUNKS))] * 4
        + [dma((ring - 1,))] * 2
        + [dma((ring - 1,))] * 4
        + [dma((ring, max(lines - 1, 1)))] * 4
        + [dma((ring, lines))] * 4,
        compiler_params=pltpu.CompilerParams(
            collective_id=0, has_side_effects=True, vmem_limit_bytes=32 << 20
        ),
        name="gather_inputs",
    )(weight, users, keys)


def share_kernel(groups, ring, x_in, x_out, own_sem, send_sem, recv_sem):
    total = groups * ring
    me = lax.axis_index("dp") * ring + lax.axis_index("fsdp")
    greet_all(groups, ring, me)

    def push(k):
        peer = lax.rem(me + k, total)
        return remote(
            x_in, x_out.at[me], send_sem.at[k - 1], recv_sem.at[k - 1],
            (peer // ring, lax.rem(peer, ring)),
        )

    def pull(k):
        source = lax.rem(me + total - k, total)
        return remote(
            x_in, x_out.at[source], send_sem.at[k - 1], recv_sem.at[k - 1],
            (source // ring, lax.rem(source, ring)),
        )

    def start(k, carry):
        push(k).start()
        return carry

    def finish(k, carry):
        push(k).wait_send()
        pull(k).wait_recv()
        return carry

    lax.fori_loop(1, total, start, 0)
    own = pltpu.make_async_copy(x_in, x_out.at[me], own_sem)
    own.start()
    own.wait()
    lax.fori_loop(1, total, finish, 0)


def share(groups, ring, block):
    total = groups * ring
    dma = pltpu.SemaphoreType.DMA
    vmem = pl.BlockSpec(memory_space=pltpu.VMEM)
    return pl.pallas_call(
        functools.partial(share_kernel, groups, ring),
        out_shape=jax.ShapeDtypeStruct((total,) + block.shape, block.dtype),
        in_specs=[vmem],
        out_specs=vmem,
        scratch_shapes=[dma, dma((total - 1,)), dma((total - 1,))],
        compiler_params=pltpu.CompilerParams(collective_id=1, has_side_effects=True),
        name="share",
    )(block)


def reduce_kernel(
    groups, ring, part_in, gain_in, out, gain_out,
    cross, held, arrived, totals, lent, borrowed,
    own_sem, g_send, g_recv, x_send, x_recv, r_send, r_recv, t_send, t_recv, o_send, o_recv,
    y_send, y_recv, f_send, f_recv,
):
    total = groups * ring
    group, index = lax.axis_index("dp"), lax.axis_index("fsdp")
    me = group * ring + index
    core = lax.rem(group, 2)
    partner = group + 1 - 2 * core
    step = 1 - 2 * core
    place = ring_place(index, ring)
    rows = part_in.shape[0] // ring
    half = rows // 2
    piece = half // CHUNKS
    lines = groups // 2
    line = group // 2
    split = lines == 2
    slots = CHUNKS - 1 if split else CHUNKS
    across = lax.rem(group + 2, groups)
    following = ring_index(lax.rem(place + ring + step, ring), ring)

    def owner(s, way=step):
        return ring_index(lax.rem(place + ring * ring - (s + 1) * way, ring), ring)

    def chunk(j):
        if not split or j < CHUNKS - 2:
            return j
        return CHUNKS - 2 + (line if j == CHUNKS - 2 else 1 - line)

    greet_all(groups, ring, me)

    def cross_out(s):
        who = owner(s, -step)
        start = pl.multiple_of(who * rows + (1 - core) * half, half)
        return remote(
            part_in.at[pl.ds(start, half), :], cross.at[s], x_send.at[s], x_recv.at[s],
            (partner, index),
        )

    def start_cross(s, carry):
        cross_out(s).start()
        return carry

    lax.fori_loop(0, ring, start_cross, 0)

    def gain_push(k):
        peer = lax.rem(me + k, total)
        return remote(
            gain_in, gain_out.at[me], g_send.at[k - 1], g_recv.at[k - 1],
            (peer // ring, lax.rem(peer, ring)),
        )

    def gain_pull(k):
        source = lax.rem(me + total - k, total)
        return remote(
            gain_in, gain_out.at[source], g_send.at[k - 1], g_recv.at[k - 1],
            (source // ring, lax.rem(source, ring)),
        )

    def start_gain(k, carry):
        gain_push(k).start()
        return carry

    lax.fori_loop(1, total, start_gain, 0)
    own = pltpu.make_async_copy(gain_in, gain_out.at[me], own_sem)
    own.start()

    def ring_copy(s, c):
        at = pl.ds(c * piece, piece)
        return remote(
            held.at[s, at, :], arrived.at[s, at, :], r_send.at[s, c], r_recv.at[s, c],
            (group, following),
        )

    def local_term(s, j):
        offset = chunk(j) * piece
        start = pl.multiple_of(owner(s) * rows + core * half + offset, piece)
        mine = part_in[pl.ds(start, piece), :].astype(jnp.float32)
        return mine + cross[s, pl.ds(pl.multiple_of(offset, piece), piece), :].astype(jnp.float32)

    def lend(s):
        return remote(lent.at[s], borrowed.at[s], y_send.at[s], y_recv.at[s], (across, index))

    def prepare(s):
        cross_out(s).wait_recv()
        if split:
            lent[s] = local_term(s, CHUNKS - 1).astype(lent.dtype)
            lend(s).start()

    def term_of(s, j):
        term = local_term(s, j)
        if split and j == CHUNKS - 2:
            lend(s).wait_recv()
            term = term + borrowed[s].astype(jnp.float32)
        return term

    prepare(0)
    for j in range(slots):
        if j == CHUNKS - 2:
            prepare(1)
        held[0, pl.ds(j * piece, piece), :] = term_of(0, j).astype(held.dtype)
        ring_copy(0, j).start()

    def pass_on(s, carry):
        for j in range(slots):
            at = pl.ds(j * piece, piece)
            if j == CHUNKS - 2:
                prepare(s + 1)
            term = term_of(s, j)
            ring_copy(s - 1, j).wait_recv()
            held[s, at, :] = (term + arrived[s - 1, at, :].astype(jnp.float32)).astype(held.dtype)
            ring_copy(s, j).start()
        return carry

    lax.fori_loop(1, ring - 1, pass_on, 0)
    last = ring - 1

    def total_copy(k, j):
        ref = totals.at[line, pl.ds(j * piece, piece), :]
        return remote(
            ref, ref, t_send.at[k - 1, j], t_recv.at[k - 1, j],
            (lax.rem(group + 2 * k, groups), index),
        )

    def total_in(k, j):
        source = lax.rem(group + groups - 2 * k, groups)
        ref = totals.at[source // 2, pl.ds(j * piece, piece), :]
        return remote(ref, ref, t_send.at[k - 1, j], t_recv.at[k - 1, j], (source, index))

    def out_rows(j, side=core):
        return pl.ds(pl.multiple_of(side * half + chunk(j) * piece, piece), piece)

    def out_copy(j, side):
        ref = out.at[out_rows(j, side), :]
        return remote(ref, ref, o_send.at[j], o_recv.at[j], (partner, index))

    def out_across(j):
        ref = out.at[out_rows(j), :]
        return remote(ref, ref, f_send.at[0], f_recv.at[0], (across, index))

    shared = range(CHUNKS - 2) if split else range(CHUNKS)
    for j in range(slots):
        at = pl.ds(j * piece, piece)
        term = term_of(last, j)
        ring_copy(last - 1, j).wait_recv()
        value = (term + arrived[last - 1, at, :].astype(jnp.float32)).astype(totals.dtype)
        if j in shared:
            totals[line, at, :] = value
            for k in range(1, lines):
                total_copy(k, j).start()
        else:
            out[out_rows(j), :] = value
            out_across(j).start()
            out_copy(j, core).start()

    for j in shared:
        at = pl.ds(j * piece, piece)
        for k in range(1, lines):
            total_in(k, j).wait_recv()
        value = totals[0, at, :].astype(jnp.float32)
        for other in range(1, lines):
            value = value + totals[other, at, :].astype(jnp.float32)
        out[out_rows(j), :] = value.astype(out.dtype)
        out_copy(j, core).start()
    if split:
        out_across(CHUNKS - 1).wait_recv()
        out_copy(CHUNKS - 1, core).start()

    def finish_cross(s, carry):
        cross_out(s).wait_send()
        if split:
            lend(s).wait_send()
        return carry

    lax.fori_loop(0, ring, finish_cross, 0)

    def finish_ring(s, carry):
        for j in range(slots):
            ring_copy(s, j).wait_send()
        return carry

    lax.fori_loop(0, ring - 1, finish_ring, 0)
    own.wait()

    def finish_gain(k, carry):
        gain_push(k).wait_send()
        gain_pull(k).wait_recv()
        return carry

    lax.fori_loop(1, total, finish_gain, 0)
    for j in shared:
        for k in range(1, lines):
            total_copy(k, j).wait_send()
    for j in range(CHUNKS):
        out_copy(j, core).wait_send()
        out_copy(j, 1 - core).wait_recv()
    if split:
        out_across(CHUNKS - 2).wait_send()


def reduce_weight(groups, ring, partial, gain):
    total = groups * ring
    rows = partial.shape[0] // ring
    half, width = rows // 2, partial.shape[1]
    dma = pltpu.SemaphoreType.DMA
    vmem = pl.BlockSpec(memory_space=pltpu.VMEM)
    return pl.pallas_call(
        functools.partial(reduce_kernel, groups, ring),
        out_shape=(
            jax.ShapeDtypeStruct((rows, width), partial.dtype),
            jax.ShapeDtypeStruct((total,) + gain.shape, gain.dtype),
        ),
        in_specs=[vmem, vmem],
        out_specs=(vmem, vmem),
        scratch_shapes=[
            pltpu.VMEM((ring, half, width), partial.dtype),
            pltpu.VMEM((ring - 1, half, width), partial.dtype),
            pltpu.VMEM((ring - 1, half, width), partial.dtype),
            pltpu.VMEM((groups // 2, half, width), partial.dtype),
            pltpu.VMEM((ring, half // CHUNKS, width), partial.dtype),
            pltpu.VMEM((ring, half // CHUNKS, width), partial.dtype),
            dma,
            dma((total - 1,)),
            dma((total - 1,)),
            dma((ring,)),
            dma((ring,)),
            dma((ring - 1, CHUNKS)),
            dma((ring - 1, CHUNKS)),
            dma((max(groups // 2 - 1, 1), CHUNKS)),
            dma((max(groups // 2 - 1, 1), CHUNKS)),
            dma((CHUNKS,)),
            dma((CHUNKS,)),
            dma((ring,)),
            dma((ring,)),
            dma((1,)),
            dma((1,)),
        ],
        compiler_params=pltpu.CompilerParams(
            collective_id=2, has_side_effects=True, vmem_limit_bytes=40 << 20
        ),
        name="reduce_weight",
    )(partial, gain)


def on_device(
    groups, ring,
    context, residual, out_weight, norm_gain, user_vectors, positive, item_ids, item_counts, lengths
):
    tok_rows, head_width = context.shape
    model_width = residual.shape[1]
    items_here = lengths.shape[0]
    item_length = tok_rows // items_here
    users_here = user_vectors.shape[0]
    devices_all = groups * ring
    lanes = 128 * pl.cdiv(max(users_here, items_here), 128)
    keys = jnp.stack(
        [jnp.pad(row, (0, lanes - row.shape[0])) for row in (positive, item_ids, item_counts)]
    )
    keys = jnp.pad(keys, ((0, 5), (0, 0)))
    weight_all, users_all, keys_all = gather_inputs(groups, ring, out_weight, user_vectors, keys)
    users_all = users_all.reshape(devices_all * users_here, model_width)
    positive_all = keys_all[:, 0, :users_here].reshape(-1)
    ids_all = keys_all[:, 1, :items_here].reshape(-1)
    counts_all = keys_all[:, 2, :items_here].reshape(-1)
    attended = jnp.dot(context, weight_all, preferred_element_type=jnp.float32)
    stream = residual.astype(jnp.float32) + attended
    inverse_root_mean = lax.rsqrt(jnp.mean(stream * stream, axis=-1, keepdims=True) + EPSILON)
    normed = stream * inverse_root_mean * norm_gain
    positions = jnp.arange(item_length, dtype=jnp.int32)
    inside = (positions[None, :] < lengths[:, None])[:, :, None]
    length_float = lengths.astype(jnp.float32)[:, None]
    normed_items = normed.reshape(items_here, item_length, model_width)
    pooled = jnp.sum(jnp.where(inside, normed_items, 0.0), axis=1) / length_float
    emb_scale = lax.rsqrt(jnp.mean(pooled * pooled, axis=-1, keepdims=True) + EPSILON)
    embedding = (pooled * emb_scale).astype(jnp.bfloat16)
    emb_all = share(groups, ring, embedding).reshape(devices_all * items_here, model_width)
    me = lax.axis_index("dp") * ring + lax.axis_index("fsdp")
    items_all = jnp.arange(ids_all.shape[0], dtype=jnp.int32)
    onehot = items_all[None, :] == positive_all[:, None]
    positive_id = jnp.sum(jnp.where(onehot, ids_all[None, :], 0), axis=1)
    excluded = (ids_all[None, :] == positive_id[:, None]) & jnp.logical_not(onehot)
    scores = contract_last(users_all, emb_all)
    log_counts = jnp.log(counts_all.astype(jnp.float32))
    logits = jnp.where(excluded, MASKED_FILL, scores - log_counts[None, :])
    row_max = jnp.max(logits, axis=1, keepdims=True)
    weights = jnp.where(excluded, 0.0, jnp.exp(logits - row_max))
    row_total = jnp.sum(weights, axis=1, keepdims=True)
    log_total = row_max[:, 0] + jnp.log(row_total[:, 0])
    mean_loss = jnp.mean(log_total - jnp.sum(jnp.where(onehot, logits, 0.0), axis=1))
    logit_grad = (weights / row_total - onehot.astype(jnp.float32)).astype(jnp.bfloat16)
    own_users = lax.dynamic_slice_in_dim(logit_grad, me * users_here, users_here, axis=0)
    user_grad = jnp.dot(own_users, emb_all, preferred_element_type=jnp.float32).astype(
        jnp.bfloat16
    )
    own_items = lax.dynamic_slice_in_dim(logit_grad, me * items_here, items_here, axis=1)
    emb_grad = contract_rows(own_items, users_all)
    pooled_grad = emb_scale * emb_grad - pooled * emb_scale**3 * jnp.mean(
        pooled * emb_grad, axis=-1, keepdims=True
    )
    normed_grad = jnp.where(inside, pooled_grad[:, None, :] / length_float[:, :, None], 0.0)
    normed_grad = normed_grad.reshape(tok_rows, model_width)
    gain_part = jnp.sum(normed_grad * stream * inverse_root_mean, axis=0)
    scaled = norm_gain * normed_grad
    stream_grad = inverse_root_mean * scaled - stream * inverse_root_mean**3 * jnp.mean(
        scaled * stream, axis=-1, keepdims=True
    )
    residual_grad = stream_grad.astype(jnp.bfloat16)
    context_grad = contract_last(residual_grad, weight_all).astype(jnp.bfloat16)
    partial = contract_rows(context, residual_grad).astype(jnp.bfloat16)
    weight_grad, gain_all = reduce_weight(groups, ring, partial, gain_part[None, :])
    gain_grad = jnp.sum(gain_all[:, 0, :], axis=0)
    return (mean_loss, residual_grad, context_grad, weight_grad, gain_grad, user_grad)


def solution(mesh):
    placed = (
        P(("dp", "fsdp"), None),
        P(("dp", "fsdp"), None),
        P("fsdp", None),
        P(),
        P(("dp", "fsdp"), None),
        P(("dp", "fsdp")),
        P(("dp", "fsdp")),
        P(("dp", "fsdp")),
        P(("dp", "fsdp")),
    )
    return jax.shard_map(
        functools.partial(on_device, mesh.shape["dp"], mesh.shape["fsdp"]),
        mesh=mesh,
        in_specs=placed,
        out_specs=(
            P(),
            P(("dp", "fsdp"), None),
            P(("dp", "fsdp"), None),
            P("fsdp", None),
            P(),
            P(("dp", "fsdp"), None),
        ),
        check_vma=False,
    )
```

```python
import functools

import jax
import jax.numpy as jnp
from jax import lax
from jax.experimental import pallas as pl
from jax.experimental.pallas import tpu as pltpu
from jax.sharding import PartitionSpec as P

EPSILON = 1e-06
MASKED_FILL = -1e30
MESH = pl.DeviceIdType.MESH
CHUNKS = 4


def contract_rows(left, right):
    return lax.dot_general(
        left, right, (((0,), (0,)), ((), ())), preferred_element_type=jnp.float32
    )


def contract_last(left, right):
    return lax.dot_general(
        left, right, (((1,), (1,)), ((), ())), preferred_element_type=jnp.float32
    )


def ring_place(index, count):
    return jnp.where(index % 2 == 0, index // 2, count - 1 - index // 2)


def ring_index(place, count):
    return jnp.where(place < count // 2, 2 * place, 2 * (count - 1 - place) + 1)


def greet(devices):
    barrier = pltpu.get_barrier_semaphore()
    for device in devices:
        pl.semaphore_signal(barrier, inc=1, device_id=device, device_id_type=MESH)
    pl.semaphore_wait(barrier, len(devices))


def greet_all(groups, ring, me):
    total = groups * ring
    barrier = pltpu.get_barrier_semaphore()

    def signal(k, carry):
        peer = lax.rem(me + k, total)
        pl.semaphore_signal(
            barrier, inc=1, device_id=(peer // ring, lax.rem(peer, ring)), device_id_type=MESH
        )
        return carry

    lax.fori_loop(1, total, signal, 0)
    pl.semaphore_wait(barrier, total - 1)


def remote(src, dst, send_sem, recv_sem, device):
    return pltpu.make_async_remote_copy(
        src_ref=src,
        dst_ref=dst,
        send_sem=send_sem,
        recv_sem=recv_sem,
        device_id=device,
        device_id_type=MESH,
    )


def gather_kernel(
    groups, ring, w_in, u_in, k_in, w_out, u_out, k_out,
    own_sem, w_send, w_recv, p_send, p_recv, y_send, y_recv,
    u_send, u_recv, k_send, k_recv, ul_send, ul_recv, kl_send, kl_recv,
    up_send, up_recv, kp_send, kp_recv,
):
    group, index = lax.axis_index("dp"), lax.axis_index("fsdp")
    lines = groups // 2
    split = lines == 2
    slots = CHUNKS - 1 if split else CHUNKS
    line = group // 2
    core = lax.rem(group, 2)
    partner = group + 1 - 2 * core
    across = lax.rem(group + 2, groups)
    place = ring_place(index, ring)
    ends = (
        ring_index(lax.rem(place + 1, ring), ring),
        ring_index(lax.rem(place + ring - 1, ring), ring),
    )
    rows = w_in.shape[0]
    half = rows // 2
    part = half // CHUNKS
    hops = ring - 1

    def owner(m):
        if m == hops + 2:
            return index
        away = -(m // 2) if m % 2 == 0 else m // 2
        return ring_index(lax.rem(place + ring + away, ring), ring)

    def chunk(j):
        if not split or j < CHUNKS - 2:
            return j
        return CHUNKS - 2 + (line if j == CHUNKS - 2 else 1 - line)

    def w_slice(who, j, side=core):
        start = pl.multiple_of(who * rows + side * half + chunk(j) * part, part)
        return w_out.at[pl.ds(start, part), :]

    greet(
        [(lax.rem(group + k, groups), index) for k in range(1, groups)]
        + [(group, end) for end in ends]
    )
    own = [
        pltpu.make_async_copy(
            w_in, w_out.at[pl.ds(pl.multiple_of(index * rows, rows), rows), :], own_sem.at[0]
        ),
        pltpu.make_async_copy(u_in, u_out.at[group * ring + index], own_sem.at[1]),
        pltpu.make_async_copy(k_in, k_out.at[group * ring + index], own_sem.at[2]),
    ]
    for copy in own:
        copy.start()
    for copy in own:
        copy.wait()

    def w_ring(m, j, shift=0):
        ref = w_slice(owner(m + shift), j)
        return remote(ref, ref, w_send.at[m, j], w_recv.at[m, j], (group, ends[m % 2]))

    def w_part(m, j, side=core):
        ref = w_slice(owner(m + 2), j, side)
        return remote(ref, ref, p_send.at[m, j], p_recv.at[m, j], (partner, index))

    def w_across(m, j):
        ref = w_slice(owner(m + 2), j)
        return remote(ref, ref, y_send.at[m], y_recv.at[m], (across, index))

    small = (
        (u_out, u_send, u_recv, ul_send, ul_recv, up_send, up_recv),
        (k_out, k_send, k_recv, kl_send, kl_recv, kp_send, kp_recv),
    )

    def s_ring(a, m, shift):
        out, send, recv = small[a][:3]
        ref = out.at[group * ring + owner(m + shift)]
        return remote(ref, ref, send.at[m], recv.at[m], (group, ends[m % 2]))

    def s_line(a, s, k):
        out, _, _, send, recv = small[a][:5]
        ref = out.at[group * ring + owner(s + 2)]
        peer = lax.rem(group + 2 * k, groups)
        return remote(ref, ref, send.at[s, k - 1], recv.at[s, k - 1], (peer, index))

    def s_line_in(a, s, k):
        out, _, _, send, recv = small[a][:5]
        source = lax.rem(group + groups - 2 * k, groups)
        ref = out.at[source * ring + owner(s + 2)]
        return remote(ref, ref, send.at[s, k - 1], recv.at[s, k - 1], (source, index))

    def s_part(a, s, k):
        out, send, recv = small[a][0], small[a][5], small[a][6]
        source = lax.rem(group + groups - 2 * k, groups)
        ref = out.at[source * ring + owner(s + 2)]
        return remote(ref, ref, send.at[s, k], recv.at[s, k], (partner, index))

    def s_part_in(a, s, k):
        out, send, recv = small[a][0], small[a][5], small[a][6]
        source = lax.rem(partner + groups - 2 * k, groups)
        ref = out.at[source * ring + owner(s + 2)]
        return remote(ref, ref, send.at[s, k], recv.at[s, k], (partner, index))

    def w_pass(s):
        if split:
            w_across(s, CHUNKS - 1).wait_recv()
            w_part(s, CHUNKS - 1).start()

    def spread(s):
        for a in (0, 1):
            for k in range(1, lines):
                s_line(a, s, k).start()
            s_part(a, s, 0).start()

    def s_pass(s):
        for a in (0, 1):
            for k in range(1, lines):
                s_line_in(a, s, k).wait_recv()
                s_part(a, s, k).start()

    for m in range(min(2, hops)):
        for j in range(slots):
            w_ring(m, j).start()
    for m in range(min(2, hops)):
        for a in (0, 1):
            s_ring(a, m, 0).start()
    spread(hops)
    for m in range(hops):
        more = m + 2 < hops
        for j in range(slots):
            w_ring(m, j, 2).wait_recv()
            if more:
                w_ring(m + 2, j).start()
            if split and j == CHUNKS - 2:
                w_across(m, j).start()
            w_part(m, j).start()
        for a in (0, 1):
            s_ring(a, m, 2).wait_recv()
            if more:
                s_ring(a, m + 2, 0).start()
        spread(m)
        if m == 1:
            s_pass(hops)
        if m >= 2:
            w_pass(m - 2)
            s_pass(m - 2)
    for m in range(hops - 2, hops):
        w_pass(m)
        s_pass(m)
    for m in range(hops):
        for j in range(slots):
            w_ring(m, j).wait_send()
        if split:
            w_across(m, CHUNKS - 2).wait_send()
        for j in range(CHUNKS):
            w_part(m, j).wait_send()
            w_part(m, j, 1 - core).wait_recv()
        for a in (0, 1):
            s_ring(a, m, 0).wait_send()
    for m in range(ring):
        for a in (0, 1):
            for k in range(1, lines):
                s_line(a, m, k).wait_send()
            for k in range(lines):
                s_part(a, m, k).wait_send()
                s_part_in(a, m, k).wait_recv()


def gather_inputs(groups, ring, weight, users, keys):
    total = groups * ring
    lines = groups // 2
    rows, width = weight.shape
    dma = pltpu.SemaphoreType.DMA
    vmem = pl.BlockSpec(memory_space=pltpu.VMEM)
    anywhere = pl.BlockSpec(memory_space=pl.ANY)
    return pl.pallas_call(
        functools.partial(gather_kernel, groups, ring),
        out_shape=(
            jax.ShapeDtypeStruct((ring * rows, width), weight.dtype),
            jax.ShapeDtypeStruct((total,) + users.shape, users.dtype),
            jax.ShapeDtypeStruct((total,) + keys.shape, keys.dtype),
        ),
        in_specs=[anywhere, anywhere, anywhere],
        out_specs=(vmem, vmem, vmem),
        scratch_shapes=[dma((3,))]
        + [dma((ring - 1, CHUNKS))] * 4
        + [dma((ring - 1,))] * 2
        + [dma((ring - 1,))] * 4
        + [dma((ring, max(lines - 1, 1)))] * 4
        + [dma((ring, lines))] * 4,
        compiler_params=pltpu.CompilerParams(
            collective_id=0, has_side_effects=True, vmem_limit_bytes=32 << 20
        ),
        name="gather_inputs",
    )(weight, users, keys)


def share_kernel(groups, ring, x_in, x_out, own_sem, send_sem, recv_sem):
    total = groups * ring
    me = lax.axis_index("dp") * ring + lax.axis_index("fsdp")
    greet_all(groups, ring, me)

    def push(k):
        peer = lax.rem(me + k, total)
        return remote(
            x_in, x_out.at[me], send_sem.at[k - 1], recv_sem.at[k - 1],
            (peer // ring, lax.rem(peer, ring)),
        )

    def pull(k):
        source = lax.rem(me + total - k, total)
        return remote(
            x_in, x_out.at[source], send_sem.at[k - 1], recv_sem.at[k - 1],
            (source // ring, lax.rem(source, ring)),
        )

    def start(k, carry):
        push(k).start()
        return carry

    def finish(k, carry):
        push(k).wait_send()
        pull(k).wait_recv()
        return carry

    lax.fori_loop(1, total, start, 0)
    own = pltpu.make_async_copy(x_in, x_out.at[me], own_sem)
    own.start()
    own.wait()
    lax.fori_loop(1, total, finish, 0)


def share(groups, ring, block):
    total = groups * ring
    dma = pltpu.SemaphoreType.DMA
    vmem = pl.BlockSpec(memory_space=pltpu.VMEM)
    return pl.pallas_call(
        functools.partial(share_kernel, groups, ring),
        out_shape=jax.ShapeDtypeStruct((total,) + block.shape, block.dtype),
        in_specs=[vmem],
        out_specs=vmem,
        scratch_shapes=[dma, dma((total - 1,)), dma((total - 1,))],
        compiler_params=pltpu.CompilerParams(collective_id=1, has_side_effects=True),
        name="share",
    )(block)


def reduce_kernel(
    groups, ring, part_in, gain_in, out, gain_out,
    cross, held, arrived, totals, lent, borrowed,
    own_sem, g_send, g_recv, x_send, x_recv, r_send, r_recv, t_send, t_recv, o_send, o_recv,
    y_send, y_recv, f_send, f_recv,
):
    total = groups * ring
    group, index = lax.axis_index("dp"), lax.axis_index("fsdp")
    me = group * ring + index
    core = lax.rem(group, 2)
    partner = group + 1 - 2 * core
    place = ring_place(index, ring)
    ends = (
        ring_index(lax.rem(place + 1, ring), ring),
        ring_index(lax.rem(place + ring - 1, ring), ring),
    )
    hops = ring - 1
    rows = part_in.shape[0] // ring
    half = rows // 2
    piece = half // CHUNKS
    lines = groups // 2
    line = group // 2
    split = lines == 2
    slots = CHUNKS - 1 if split else CHUNKS
    across = lax.rem(group + 2, groups)

    def owner(m):
        if m == hops:
            return index
        away = ring // 2 - m // 2 if m % 2 == 0 else m // 2 - (ring - 1) // 2
        return ring_index(lax.rem(place + ring + away, ring), ring)

    def chunk(j):
        if not split or j < CHUNKS - 2:
            return j
        return CHUNKS - 2 + (line if j == CHUNKS - 2 else 1 - line)

    greet_all(groups, ring, me)

    def cross_out(m):
        start = pl.multiple_of(owner(m) * rows + (1 - core) * half, half)
        return remote(
            part_in.at[pl.ds(start, half), :], cross.at[m], x_send.at[m], x_recv.at[m],
            (partner, index),
        )

    for m in range(ring):
        cross_out(m).start()

    def gain_push(k):
        peer = lax.rem(me + k, total)
        return remote(
            gain_in, gain_out.at[me], g_send.at[k - 1], g_recv.at[k - 1],
            (peer // ring, lax.rem(peer, ring)),
        )

    def gain_pull(k):
        source = lax.rem(me + total - k, total)
        return remote(
            gain_in, gain_out.at[source], g_send.at[k - 1], g_recv.at[k - 1],
            (source // ring, lax.rem(source, ring)),
        )

    def start_gain(k, carry):
        gain_push(k).start()
        return carry

    lax.fori_loop(1, total, start_gain, 0)
    own = pltpu.make_async_copy(gain_in, gain_out.at[me], own_sem)
    own.start()

    def ring_copy(s, c):
        at = pl.ds(c * piece, piece)
        return remote(
            held.at[s, at, :], arrived.at[s, at, :], r_send.at[s, c], r_recv.at[s, c],
            (group, ends[s % 2]),
        )

    def local_term(s, j):
        offset = chunk(j) * piece
        start = pl.multiple_of(owner(s) * rows + core * half + offset, piece)
        mine = part_in[pl.ds(start, piece), :].astype(jnp.float32)
        return mine + cross[s, pl.ds(pl.multiple_of(offset, piece), piece), :].astype(jnp.float32)

    def lend(s):
        return remote(lent.at[s], borrowed.at[s], y_send.at[s], y_recv.at[s], (across, index))

    def prepare(s):
        cross_out(s).wait_recv()
        if split:
            lent[s] = local_term(s, CHUNKS - 1).astype(lent.dtype)
            lend(s).start()

    def term_of(s, j):
        term = local_term(s, j)
        if split and j == CHUNKS - 2:
            lend(s).wait_recv()
            term = term + borrowed[s].astype(jnp.float32)
        return term

    for m in range(min(2, hops)):
        prepare(m)
    for m in range(hops):
        for j in range(slots):
            at = pl.ds(j * piece, piece)
            if j == max(CHUNKS - 2, 0) and m + 2 < ring:
                prepare(m + 2)
            term = term_of(m, j)
            if m >= 2:
                ring_copy(m - 2, j).wait_recv()
                term = term + arrived[m - 2, at, :].astype(jnp.float32)
            held[m, at, :] = term.astype(held.dtype)
            ring_copy(m, j).start()
    last = hops

    def total_copy(k, j):
        ref = totals.at[line, pl.ds(j * piece, piece), :]
        return remote(
            ref, ref, t_send.at[k - 1, j], t_recv.at[k - 1, j],
            (lax.rem(group + 2 * k, groups), index),
        )

    def total_in(k, j):
        source = lax.rem(group + groups - 2 * k, groups)
        ref = totals.at[source // 2, pl.ds(j * piece, piece), :]
        return remote(ref, ref, t_send.at[k - 1, j], t_recv.at[k - 1, j], (source, index))

    def out_rows(j, side=core):
        return pl.ds(pl.multiple_of(side * half + chunk(j) * piece, piece), piece)

    def out_copy(j, side):
        ref = out.at[out_rows(j, side), :]
        return remote(ref, ref, o_send.at[j], o_recv.at[j], (partner, index))

    def out_across(j):
        ref = out.at[out_rows(j), :]
        return remote(ref, ref, f_send.at[0], f_recv.at[0], (across, index))

    shared = range(CHUNKS - 2) if split else range(CHUNKS)
    for j in range(slots):
        at = pl.ds(j * piece, piece)
        term = term_of(last, j)
        for m in range(max(hops - 2, 0), hops):
            ring_copy(m, j).wait_recv()
            term = term + arrived[m, at, :].astype(jnp.float32)
        value = term.astype(totals.dtype)
        if j in shared:
            totals[line, at, :] = value
            for k in range(1, lines):
                total_copy(k, j).start()
        else:
            out[out_rows(j), :] = value
            out_across(j).start()
            out_copy(j, core).start()

    for j in shared:
        at = pl.ds(j * piece, piece)
        for k in range(1, lines):
            total_in(k, j).wait_recv()
        value = totals[0, at, :].astype(jnp.float32)
        for other in range(1, lines):
            value = value + totals[other, at, :].astype(jnp.float32)
        out[out_rows(j), :] = value.astype(out.dtype)
        out_copy(j, core).start()
    if split:
        out_across(CHUNKS - 1).wait_recv()
        out_copy(CHUNKS - 1, core).start()

    for m in range(ring):
        cross_out(m).wait_send()
        if split:
            lend(m).wait_send()
    for m in range(hops):
        for j in range(slots):
            ring_copy(m, j).wait_send()
    own.wait()

    def finish_gain(k, carry):
        gain_push(k).wait_send()
        gain_pull(k).wait_recv()
        return carry

    lax.fori_loop(1, total, finish_gain, 0)
    for j in shared:
        for k in range(1, lines):
            total_copy(k, j).wait_send()
    for j in range(CHUNKS):
        out_copy(j, core).wait_send()
        out_copy(j, 1 - core).wait_recv()
    if split:
        out_across(CHUNKS - 2).wait_send()


def reduce_weight(groups, ring, partial, gain):
    total = groups * ring
    rows = partial.shape[0] // ring
    half, width = rows // 2, partial.shape[1]
    dma = pltpu.SemaphoreType.DMA
    vmem = pl.BlockSpec(memory_space=pltpu.VMEM)
    return pl.pallas_call(
        functools.partial(reduce_kernel, groups, ring),
        out_shape=(
            jax.ShapeDtypeStruct((rows, width), partial.dtype),
            jax.ShapeDtypeStruct((total,) + gain.shape, gain.dtype),
        ),
        in_specs=[vmem, vmem],
        out_specs=(vmem, vmem),
        scratch_shapes=[
            pltpu.VMEM((ring, half, width), partial.dtype),
            pltpu.VMEM((ring - 1, half, width), partial.dtype),
            pltpu.VMEM((ring - 1, half, width), partial.dtype),
            pltpu.VMEM((groups // 2, half, width), partial.dtype),
            pltpu.VMEM((ring, half // CHUNKS, width), partial.dtype),
            pltpu.VMEM((ring, half // CHUNKS, width), partial.dtype),
            dma,
            dma((total - 1,)),
            dma((total - 1,)),
            dma((ring,)),
            dma((ring,)),
            dma((ring - 1, CHUNKS)),
            dma((ring - 1, CHUNKS)),
            dma((max(groups // 2 - 1, 1), CHUNKS)),
            dma((max(groups // 2 - 1, 1), CHUNKS)),
            dma((CHUNKS,)),
            dma((CHUNKS,)),
            dma((ring,)),
            dma((ring,)),
            dma((1,)),
            dma((1,)),
        ],
        compiler_params=pltpu.CompilerParams(
            collective_id=2, has_side_effects=True, vmem_limit_bytes=40 << 20
        ),
        name="reduce_weight",
    )(partial, gain)


def on_device(
    groups, ring,
    context, residual, out_weight, norm_gain, user_vectors, positive, item_ids, item_counts, lengths
):
    tok_rows, head_width = context.shape
    model_width = residual.shape[1]
    items_here = lengths.shape[0]
    item_length = tok_rows // items_here
    users_here = user_vectors.shape[0]
    devices_all = groups * ring
    lanes = 128 * pl.cdiv(max(users_here, items_here), 128)
    keys = jnp.stack(
        [jnp.pad(row, (0, lanes - row.shape[0])) for row in (positive, item_ids, item_counts)]
    )
    keys = jnp.pad(keys, ((0, 5), (0, 0)))
    weight_all, users_all, keys_all = gather_inputs(groups, ring, out_weight, user_vectors, keys)
    users_all = users_all.reshape(devices_all * users_here, model_width)
    positive_all = keys_all[:, 0, :users_here].reshape(-1)
    ids_all = keys_all[:, 1, :items_here].reshape(-1)
    counts_all = keys_all[:, 2, :items_here].reshape(-1)
    attended = jnp.dot(context, weight_all, preferred_element_type=jnp.float32)
    stream = residual.astype(jnp.float32) + attended
    inverse_root_mean = lax.rsqrt(jnp.mean(stream * stream, axis=-1, keepdims=True) + EPSILON)
    normed = stream * inverse_root_mean * norm_gain
    positions = jnp.arange(item_length, dtype=jnp.int32)
    inside = (positions[None, :] < lengths[:, None])[:, :, None]
    length_float = lengths.astype(jnp.float32)[:, None]
    normed_items = normed.reshape(items_here, item_length, model_width)
    pooled = jnp.sum(jnp.where(inside, normed_items, 0.0), axis=1) / length_float
    emb_scale = lax.rsqrt(jnp.mean(pooled * pooled, axis=-1, keepdims=True) + EPSILON)
    embedding = (pooled * emb_scale).astype(jnp.bfloat16)
    emb_all = share(groups, ring, embedding).reshape(devices_all * items_here, model_width)
    me = lax.axis_index("dp") * ring + lax.axis_index("fsdp")
    items_all = jnp.arange(ids_all.shape[0], dtype=jnp.int32)
    onehot = items_all[None, :] == positive_all[:, None]
    positive_id = jnp.sum(jnp.where(onehot, ids_all[None, :], 0), axis=1)
    excluded = (ids_all[None, :] == positive_id[:, None]) & jnp.logical_not(onehot)
    scores = contract_last(users_all, emb_all)
    log_counts = jnp.log(counts_all.astype(jnp.float32))
    logits = jnp.where(excluded, MASKED_FILL, scores - log_counts[None, :])
    row_max = jnp.max(logits, axis=1, keepdims=True)
    weights = jnp.where(excluded, 0.0, jnp.exp(logits - row_max))
    row_total = jnp.sum(weights, axis=1, keepdims=True)
    log_total = row_max[:, 0] + jnp.log(row_total[:, 0])
    mean_loss = jnp.mean(log_total - jnp.sum(jnp.where(onehot, logits, 0.0), axis=1))
    logit_grad = (weights / row_total - onehot.astype(jnp.float32)).astype(jnp.bfloat16)
    own_users = lax.dynamic_slice_in_dim(logit_grad, me * users_here, users_here, axis=0)
    user_grad = jnp.dot(own_users, emb_all, preferred_element_type=jnp.float32).astype(
        jnp.bfloat16
    )
    own_items = lax.dynamic_slice_in_dim(logit_grad, me * items_here, items_here, axis=1)
    emb_grad = contract_rows(own_items, users_all)
    pooled_grad = emb_scale * emb_grad - pooled * emb_scale**3 * jnp.mean(
        pooled * emb_grad, axis=-1, keepdims=True
    )
    normed_grad = jnp.where(inside, pooled_grad[:, None, :] / length_float[:, :, None], 0.0)
    normed_grad = normed_grad.reshape(tok_rows, model_width)
    gain_part = jnp.sum(normed_grad * stream * inverse_root_mean, axis=0)
    scaled = norm_gain * normed_grad
    stream_grad = inverse_root_mean * scaled - stream * inverse_root_mean**3 * jnp.mean(
        scaled * stream, axis=-1, keepdims=True
    )
    residual_grad = stream_grad.astype(jnp.bfloat16)
    context_grad = contract_last(residual_grad, weight_all).astype(jnp.bfloat16)
    partial = contract_rows(context, residual_grad).astype(jnp.bfloat16)
    weight_grad, gain_all = reduce_weight(groups, ring, partial, gain_part[None, :])
    gain_grad = jnp.sum(gain_all[:, 0, :], axis=0)
    return (mean_loss, residual_grad, context_grad, weight_grad, gain_grad, user_grad)


def solution(mesh):
    placed = (
        P(("dp", "fsdp"), None),
        P(("dp", "fsdp"), None),
        P("fsdp", None),
        P(),
        P(("dp", "fsdp"), None),
        P(("dp", "fsdp")),
        P(("dp", "fsdp")),
        P(("dp", "fsdp")),
        P(("dp", "fsdp")),
    )
    return jax.shard_map(
        functools.partial(on_device, mesh.shape["dp"], mesh.shape["fsdp"]),
        mesh=mesh,
        in_specs=placed,
        out_specs=(
            P(),
            P(("dp", "fsdp"), None),
            P(("dp", "fsdp"), None),
            P("fsdp", None),
            P(),
            P(("dp", "fsdp"), None),
        ),
        check_vma=False,
    )
```

```python
import functools

import jax
import jax.numpy as jnp
from jax import lax
from jax.experimental import pallas as pl
from jax.experimental.pallas import tpu as pltpu
from jax.sharding import PartitionSpec as P

EPSILON = 1e-06
MASKED_FILL = -1e30
MESH = pl.DeviceIdType.MESH
CHUNKS = 4


def contract_rows(left, right):
    return lax.dot_general(
        left, right, (((0,), (0,)), ((), ())), preferred_element_type=jnp.float32
    )


def contract_last(left, right):
    return lax.dot_general(
        left, right, (((1,), (1,)), ((), ())), preferred_element_type=jnp.float32
    )


def ring_place(index, count):
    return jnp.where(index % 2 == 0, index // 2, count - 1 - index // 2)


def ring_index(place, count):
    return jnp.where(place < count // 2, 2 * place, 2 * (count - 1 - place) + 1)


def greet(devices):
    barrier = pltpu.get_barrier_semaphore()
    for device in devices:
        pl.semaphore_signal(barrier, inc=1, device_id=device, device_id_type=MESH)
    pl.semaphore_wait(barrier, len(devices))


def greet_all(groups, ring, me):
    total = groups * ring
    barrier = pltpu.get_barrier_semaphore()

    def signal(k, carry):
        peer = lax.rem(me + k, total)
        pl.semaphore_signal(
            barrier, inc=1, device_id=(peer // ring, lax.rem(peer, ring)), device_id_type=MESH
        )
        return carry

    lax.fori_loop(1, total, signal, 0)
    pl.semaphore_wait(barrier, total - 1)


def remote(src, dst, send_sem, recv_sem, device):
    return pltpu.make_async_remote_copy(
        src_ref=src,
        dst_ref=dst,
        send_sem=send_sem,
        recv_sem=recv_sem,
        device_id=device,
        device_id_type=MESH,
    )


def gather_kernel(
    groups, ring, w_in, u_in, k_in, w_out, u_out, k_out,
    own_sem, w_send, w_recv, p_send, p_recv, y_send, y_recv,
    u_send, u_recv, k_send, k_recv, ul_send, ul_recv, kl_send, kl_recv,
    up_send, up_recv, kp_send, kp_recv,
):
    group, index = lax.axis_index("dp"), lax.axis_index("fsdp")
    lines = groups // 2
    split = lines == 2
    slots = CHUNKS - 1 if split else CHUNKS
    line = group // 2
    core = lax.rem(group, 2)
    partner = group + 1 - 2 * core
    across = lax.rem(group + 2, groups)
    place = ring_place(index, ring)
    ends = (
        ring_index(lax.rem(place + 1, ring), ring),
        ring_index(lax.rem(place + ring - 1, ring), ring),
    )
    rows = w_in.shape[0]
    half = rows // 2
    part = half // CHUNKS
    hops = ring - 1

    def owner(m):
        if m == hops + 2:
            return index
        away = -(m // 2) if m % 2 == 0 else m // 2
        return ring_index(lax.rem(place + ring + away, ring), ring)

    def chunk(j):
        if not split or j < CHUNKS - 2:
            return j
        return CHUNKS - 2 + (line if j == CHUNKS - 2 else 1 - line)

    def w_slice(who, j, side=core):
        start = pl.multiple_of(who * rows + side * half + chunk(j) * part, part)
        return w_out.at[pl.ds(start, part), :]

    greet(
        [(lax.rem(group + k, groups), index) for k in range(1, groups)]
        + [(group, end) for end in ends]
    )
    own = [
        pltpu.make_async_copy(
            w_in, w_out.at[pl.ds(pl.multiple_of(index * rows, rows), rows), :], own_sem.at[0]
        ),
        pltpu.make_async_copy(u_in, u_out.at[group * ring + index], own_sem.at[1]),
        pltpu.make_async_copy(k_in, k_out.at[group * ring + index], own_sem.at[2]),
    ]
    for copy in own:
        copy.start()
    for copy in own:
        copy.wait()

    def w_ring(m, j, shift=0):
        ref = w_slice(owner(m + shift), j)
        return remote(ref, ref, w_send.at[m, j], w_recv.at[m, j], (group, ends[m % 2]))

    def w_part(m, j, side=core):
        ref = w_slice(owner(m + 2), j, side)
        return remote(ref, ref, p_send.at[m, j], p_recv.at[m, j], (partner, index))

    def w_across(m, j):
        ref = w_slice(owner(m + 2), j)
        return remote(ref, ref, y_send.at[m], y_recv.at[m], (across, index))

    small = (
        (u_out, u_send, u_recv, ul_send, ul_recv, up_send, up_recv),
        (k_out, k_send, k_recv, kl_send, kl_recv, kp_send, kp_recv),
    )

    def s_ring(a, m, shift):
        out, send, recv = small[a][:3]
        ref = out.at[group * ring + owner(m + shift)]
        return remote(ref, ref, send.at[m], recv.at[m], (group, ends[m % 2]))

    def s_line(a, s, k):
        out, _, _, send, recv = small[a][:5]
        ref = out.at[group * ring + owner(s + 2)]
        peer = lax.rem(group + 2 * k, groups)
        return remote(ref, ref, send.at[s, k - 1], recv.at[s, k - 1], (peer, index))

    def s_line_in(a, s, k):
        out, _, _, send, recv = small[a][:5]
        source = lax.rem(group + groups - 2 * k, groups)
        ref = out.at[source * ring + owner(s + 2)]
        return remote(ref, ref, send.at[s, k - 1], recv.at[s, k - 1], (source, index))

    def s_part(a, s, k):
        out, send, recv = small[a][0], small[a][5], small[a][6]
        source = lax.rem(group + groups - 2 * k, groups)
        ref = out.at[source * ring + owner(s + 2)]
        return remote(ref, ref, send.at[s, k], recv.at[s, k], (partner, index))

    def s_part_in(a, s, k):
        out, send, recv = small[a][0], small[a][5], small[a][6]
        source = lax.rem(partner + groups - 2 * k, groups)
        ref = out.at[source * ring + owner(s + 2)]
        return remote(ref, ref, send.at[s, k], recv.at[s, k], (partner, index))

    def w_pass(s):
        if split:
            w_across(s, CHUNKS - 1).wait_recv()
            w_part(s, CHUNKS - 1).start()

    def spread(s):
        for a in (0, 1):
            for k in range(1, lines):
                s_line(a, s, k).start()
            s_part(a, s, 0).start()

    def s_pass(s):
        for a in (0, 1):
            for k in range(1, lines):
                s_line_in(a, s, k).wait_recv()
                s_part(a, s, k).start()

    for m in range(min(2, hops)):
        for j in range(slots):
            w_ring(m, j).start()
    for m in range(min(2, hops)):
        for a in (0, 1):
            s_ring(a, m, 0).start()
    spread(hops)
    for m in range(hops):
        more = m + 2 < hops
        for j in range(slots):
            w_ring(m, j, 2).wait_recv()
            if more:
                w_ring(m + 2, j).start()
            if split and j == CHUNKS - 2:
                w_across(m, j).start()
            w_part(m, j).start()
        for a in (0, 1):
            s_ring(a, m, 2).wait_recv()
            if more:
                s_ring(a, m + 2, 0).start()
        spread(m)
        if m == 1:
            s_pass(hops)
        if m >= 2:
            w_pass(m - 2)
            s_pass(m - 2)
    for m in range(hops - 2, hops):
        w_pass(m)
        s_pass(m)
    for m in range(hops):
        for j in range(slots):
            w_ring(m, j).wait_send()
        if split:
            w_across(m, CHUNKS - 2).wait_send()
        for j in range(CHUNKS):
            w_part(m, j).wait_send()
            w_part(m, j, 1 - core).wait_recv()
        for a in (0, 1):
            s_ring(a, m, 0).wait_send()
    for m in range(ring):
        for a in (0, 1):
            for k in range(1, lines):
                s_line(a, m, k).wait_send()
            for k in range(lines):
                s_part(a, m, k).wait_send()
                s_part_in(a, m, k).wait_recv()


def gather_inputs(groups, ring, weight, users, keys):
    total = groups * ring
    lines = groups // 2
    rows, width = weight.shape
    dma = pltpu.SemaphoreType.DMA
    vmem = pl.BlockSpec(memory_space=pltpu.VMEM)
    anywhere = pl.BlockSpec(memory_space=pl.ANY)
    return pl.pallas_call(
        functools.partial(gather_kernel, groups, ring),
        out_shape=(
            jax.ShapeDtypeStruct((ring * rows, width), weight.dtype),
            jax.ShapeDtypeStruct((total,) + users.shape, users.dtype),
            jax.ShapeDtypeStruct((total,) + keys.shape, keys.dtype),
        ),
        in_specs=[anywhere, anywhere, anywhere],
        out_specs=(vmem, vmem, vmem),
        scratch_shapes=[dma((3,))]
        + [dma((ring - 1, CHUNKS))] * 4
        + [dma((ring - 1,))] * 2
        + [dma((ring - 1,))] * 4
        + [dma((ring, max(lines - 1, 1)))] * 4
        + [dma((ring, lines))] * 4,
        compiler_params=pltpu.CompilerParams(
            collective_id=0, has_side_effects=True, vmem_limit_bytes=32 << 20
        ),
        name="gather_inputs",
    )(weight, users, keys)


def share_kernel(groups, ring, x_in, x_out, own_sem, send_sem, recv_sem):
    total = groups * ring
    me = lax.axis_index("dp") * ring + lax.axis_index("fsdp")
    greet_all(groups, ring, me)

    def push(k):
        peer = lax.rem(me + k, total)
        return remote(
            x_in, x_out.at[me], send_sem.at[k - 1], recv_sem.at[k - 1],
            (peer // ring, lax.rem(peer, ring)),
        )

    def pull(k):
        source = lax.rem(me + total - k, total)
        return remote(
            x_in, x_out.at[source], send_sem.at[k - 1], recv_sem.at[k - 1],
            (source // ring, lax.rem(source, ring)),
        )

    def start(k, carry):
        push(k).start()
        return carry

    def finish(k, carry):
        push(k).wait_send()
        pull(k).wait_recv()
        return carry

    lax.fori_loop(1, total, start, 0)
    own = pltpu.make_async_copy(x_in, x_out.at[me], own_sem)
    own.start()
    own.wait()
    lax.fori_loop(1, total, finish, 0)


def share(groups, ring, block):
    total = groups * ring
    dma = pltpu.SemaphoreType.DMA
    vmem = pl.BlockSpec(memory_space=pltpu.VMEM)
    return pl.pallas_call(
        functools.partial(share_kernel, groups, ring),
        out_shape=jax.ShapeDtypeStruct((total,) + block.shape, block.dtype),
        in_specs=[vmem],
        out_specs=vmem,
        scratch_shapes=[dma, dma((total - 1,)), dma((total - 1,))],
        compiler_params=pltpu.CompilerParams(collective_id=1, has_side_effects=True),
        name="share",
    )(block)


def reduce_kernel(
    groups, ring, context_in, grad_in, weight_in, gain_in, out, gain_out, context_out,
    part_in, cross, held, arrived, totals, lent, borrowed,
    own_sem, g_send, g_recv, x_send, x_recv, r_send, r_recv, t_send, t_recv, o_send, o_recv,
    y_send, y_recv, f_send, f_recv,
):
    total = groups * ring
    group, index = lax.axis_index("dp"), lax.axis_index("fsdp")
    me = group * ring + index
    core = lax.rem(group, 2)
    partner = group + 1 - 2 * core
    place = ring_place(index, ring)
    ends = (
        ring_index(lax.rem(place + 1, ring), ring),
        ring_index(lax.rem(place + ring - 1, ring), ring),
    )
    hops = ring - 1
    rows = part_in.shape[0] // ring
    half = rows // 2
    piece = half // CHUNKS
    lines = groups // 2
    line = group // 2
    split = lines == 2
    slots = CHUNKS - 1 if split else CHUNKS
    across = lax.rem(group + 2, groups)

    def owner(m):
        if m == hops:
            return index
        away = ring // 2 - m // 2 if m % 2 == 0 else m // 2 - (ring - 1) // 2
        return ring_index(lax.rem(place + ring + away, ring), ring)

    def chunk(j):
        if not split or j < CHUNKS - 2:
            return j
        return CHUNKS - 2 + (line if j == CHUNKS - 2 else 1 - line)

    barrier = pltpu.get_barrier_semaphore()

    def signal(k, carry):
        peer = lax.rem(me + k, total)
        pl.semaphore_signal(
            barrier, inc=1, device_id=(peer // ring, lax.rem(peer, ring)), device_id_type=MESH
        )
        return carry

    lax.fori_loop(1, total, signal, 0)
    width = part_in.shape[1]
    wide = width // 2

    def multiply(m):
        start = pl.multiple_of(owner(m) * rows, rows)
        left = context_in[:, pl.ds(start, rows)]
        for t in range(2):
            at = pl.ds(t * wide, wide)
            part_in[pl.ds(start, rows), at] = contract_rows(left, grad_in[:, at]).astype(
                part_in.dtype
            )

    def context_tile(m):
        at = pl.ds(m * rows, rows)
        context_out[:, at] = contract_last(grad_in[...], weight_in[at, :]).astype(
            context_out.dtype
        )

    multiply(0)
    pl.semaphore_wait(barrier, total - 1)

    def cross_out(m):
        start = pl.multiple_of(owner(m) * rows + (1 - core) * half, half)
        return remote(
            part_in.at[pl.ds(start, half), :], cross.at[m], x_send.at[m], x_recv.at[m],
            (partner, index),
        )

    for m in range(ring):
        if m > 0:
            multiply(m)
        cross_out(m).start()

    def gain_push(k):
        peer = lax.rem(me + k, total)
        return remote(
            gain_in, gain_out.at[me], g_send.at[k - 1], g_recv.at[k - 1],
            (peer // ring, lax.rem(peer, ring)),
        )

    def gain_pull(k):
        source = lax.rem(me + total - k, total)
        return remote(
            gain_in, gain_out.at[source], g_send.at[k - 1], g_recv.at[k - 1],
            (source // ring, lax.rem(source, ring)),
        )

    def start_gain(k, carry):
        gain_push(k).start()
        return carry

    lax.fori_loop(1, total, start_gain, 0)
    own = pltpu.make_async_copy(gain_in, gain_out.at[me], own_sem)
    own.start()

    def ring_copy(s, c):
        at = pl.ds(c * piece, piece)
        return remote(
            held.at[s, at, :], arrived.at[s, at, :], r_send.at[s, c], r_recv.at[s, c],
            (group, ends[s % 2]),
        )

    def local_term(s, j):
        offset = chunk(j) * piece
        start = pl.multiple_of(owner(s) * rows + core * half + offset, piece)
        mine = part_in[pl.ds(start, piece), :].astype(jnp.float32)
        return mine + cross[s, pl.ds(pl.multiple_of(offset, piece), piece), :].astype(jnp.float32)

    def lend(s):
        return remote(lent.at[s], borrowed.at[s], y_send.at[s], y_recv.at[s], (across, index))

    def prepare(s):
        cross_out(s).wait_recv()
        if split:
            lent[s] = local_term(s, CHUNKS - 1).astype(lent.dtype)
            lend(s).start()

    def term_of(s, j):
        term = local_term(s, j)
        if split and j == CHUNKS - 2:
            lend(s).wait_recv()
            term = term + borrowed[s].astype(jnp.float32)
        return term

    for m in range(min(2, hops)):
        prepare(m)
    for m in range(hops):
        for j in range(slots):
            at = pl.ds(j * piece, piece)
            if j == max(CHUNKS - 2, 0) and m + 2 < ring:
                prepare(m + 2)
            term = term_of(m, j)
            if m >= 2:
                ring_copy(m - 2, j).wait_recv()
                term = term + arrived[m - 2, at, :].astype(jnp.float32)
            held[m, at, :] = term.astype(held.dtype)
            ring_copy(m, j).start()
        context_tile(m)
    last = hops

    def total_copy(k, j):
        ref = totals.at[line, pl.ds(j * piece, piece), :]
        return remote(
            ref, ref, t_send.at[k - 1, j], t_recv.at[k - 1, j],
            (lax.rem(group + 2 * k, groups), index),
        )

    def total_in(k, j):
        source = lax.rem(group + groups - 2 * k, groups)
        ref = totals.at[source // 2, pl.ds(j * piece, piece), :]
        return remote(ref, ref, t_send.at[k - 1, j], t_recv.at[k - 1, j], (source, index))

    def out_rows(j, side=core):
        return pl.ds(pl.multiple_of(side * half + chunk(j) * piece, piece), piece)

    def out_copy(j, side):
        ref = out.at[out_rows(j, side), :]
        return remote(ref, ref, o_send.at[j], o_recv.at[j], (partner, index))

    def out_across(j):
        ref = out.at[out_rows(j), :]
        return remote(ref, ref, f_send.at[0], f_recv.at[0], (across, index))

    shared = range(CHUNKS - 2) if split else range(CHUNKS)
    for j in range(slots):
        at = pl.ds(j * piece, piece)
        term = term_of(last, j)
        for m in range(max(hops - 2, 0), hops):
            ring_copy(m, j).wait_recv()
            term = term + arrived[m, at, :].astype(jnp.float32)
        value = term.astype(totals.dtype)
        if j in shared:
            totals[line, at, :] = value
            for k in range(1, lines):
                total_copy(k, j).start()
        else:
            out[out_rows(j), :] = value
            out_across(j).start()
            out_copy(j, core).start()

    context_tile(last)
    for j in shared:
        at = pl.ds(j * piece, piece)
        for k in range(1, lines):
            total_in(k, j).wait_recv()
        value = totals[0, at, :].astype(jnp.float32)
        for other in range(1, lines):
            value = value + totals[other, at, :].astype(jnp.float32)
        out[out_rows(j), :] = value.astype(out.dtype)
        out_copy(j, core).start()
    if split:
        out_across(CHUNKS - 1).wait_recv()
        out_copy(CHUNKS - 1, core).start()

    for m in range(ring):
        cross_out(m).wait_send()
        if split:
            lend(m).wait_send()
    for m in range(hops):
        for j in range(slots):
            ring_copy(m, j).wait_send()
    own.wait()

    def finish_gain(k, carry):
        gain_push(k).wait_send()
        gain_pull(k).wait_recv()
        return carry

    lax.fori_loop(1, total, finish_gain, 0)
    for j in shared:
        for k in range(1, lines):
            total_copy(k, j).wait_send()
    for j in range(CHUNKS):
        out_copy(j, core).wait_send()
        out_copy(j, 1 - core).wait_recv()
    if split:
        out_across(CHUNKS - 2).wait_send()


def reduce_weight(groups, ring, context, grad, weight, gain):
    total = groups * ring
    rows = weight.shape[0] // ring
    half, width = rows // 2, weight.shape[1]
    partial = jax.ShapeDtypeStruct(weight.shape, weight.dtype)
    dma = pltpu.SemaphoreType.DMA
    vmem = pl.BlockSpec(memory_space=pltpu.VMEM)
    return pl.pallas_call(
        functools.partial(reduce_kernel, groups, ring),
        out_shape=(
            jax.ShapeDtypeStruct((rows, width), partial.dtype),
            jax.ShapeDtypeStruct((total,) + gain.shape, gain.dtype),
            jax.ShapeDtypeStruct(context.shape, context.dtype),
        ),
        in_specs=[vmem, vmem, vmem, vmem],
        out_specs=(vmem, vmem, vmem),
        scratch_shapes=[
            pltpu.VMEM(partial.shape, partial.dtype),
            pltpu.VMEM((ring, half, width), partial.dtype),
            pltpu.VMEM((ring - 1, half, width), partial.dtype),
            pltpu.VMEM((ring - 1, half, width), partial.dtype),
            pltpu.VMEM((groups // 2, half, width), partial.dtype),
            pltpu.VMEM((ring, half // CHUNKS, width), partial.dtype),
            pltpu.VMEM((ring, half // CHUNKS, width), partial.dtype),
            dma,
            dma((total - 1,)),
            dma((total - 1,)),
            dma((ring,)),
            dma((ring,)),
            dma((ring - 1, CHUNKS)),
            dma((ring - 1, CHUNKS)),
            dma((max(groups // 2 - 1, 1), CHUNKS)),
            dma((max(groups // 2 - 1, 1), CHUNKS)),
            dma((CHUNKS,)),
            dma((CHUNKS,)),
            dma((ring,)),
            dma((ring,)),
            dma((1,)),
            dma((1,)),
        ],
        compiler_params=pltpu.CompilerParams(
            collective_id=2, has_side_effects=True, vmem_limit_bytes=40 << 20
        ),
        name="reduce_weight",
    )(context, grad, weight, gain)


def on_device(
    groups, ring,
    context, residual, out_weight, norm_gain, user_vectors, positive, item_ids, item_counts, lengths
):
    tok_rows, head_width = context.shape
    model_width = residual.shape[1]
    items_here = lengths.shape[0]
    item_length = tok_rows // items_here
    users_here = user_vectors.shape[0]
    devices_all = groups * ring
    lanes = 128 * pl.cdiv(max(users_here, items_here), 128)
    keys = jnp.stack(
        [jnp.pad(row, (0, lanes - row.shape[0])) for row in (positive, item_ids, item_counts)]
    )
    keys = jnp.pad(keys, ((0, 5), (0, 0)))
    weight_all, users_all, keys_all = gather_inputs(groups, ring, out_weight, user_vectors, keys)
    users_all = users_all.reshape(devices_all * users_here, model_width)
    positive_all = keys_all[:, 0, :users_here].reshape(-1)
    ids_all = keys_all[:, 1, :items_here].reshape(-1)
    counts_all = keys_all[:, 2, :items_here].reshape(-1)
    attended = jnp.dot(context, weight_all, preferred_element_type=jnp.float32)
    stream = residual.astype(jnp.float32) + attended
    inverse_root_mean = lax.rsqrt(jnp.mean(stream * stream, axis=-1, keepdims=True) + EPSILON)
    normed = stream * inverse_root_mean * norm_gain
    positions = jnp.arange(item_length, dtype=jnp.int32)
    inside = (positions[None, :] < lengths[:, None])[:, :, None]
    length_float = lengths.astype(jnp.float32)[:, None]
    normed_items = normed.reshape(items_here, item_length, model_width)
    pooled = jnp.sum(jnp.where(inside, normed_items, 0.0), axis=1) / length_float
    emb_scale = lax.rsqrt(jnp.mean(pooled * pooled, axis=-1, keepdims=True) + EPSILON)
    embedding = (pooled * emb_scale).astype(jnp.bfloat16)
    emb_all = share(groups, ring, embedding).reshape(devices_all * items_here, model_width)
    me = lax.axis_index("dp") * ring + lax.axis_index("fsdp")
    items_all = jnp.arange(ids_all.shape[0], dtype=jnp.int32)
    onehot = items_all[None, :] == positive_all[:, None]
    positive_id = jnp.sum(jnp.where(onehot, ids_all[None, :], 0), axis=1)
    excluded = (ids_all[None, :] == positive_id[:, None]) & jnp.logical_not(onehot)
    scores = contract_last(users_all, emb_all)
    log_counts = jnp.log(counts_all.astype(jnp.float32))
    logits = jnp.where(excluded, MASKED_FILL, scores - log_counts[None, :])
    row_max = jnp.max(logits, axis=1, keepdims=True)
    weights = jnp.where(excluded, 0.0, jnp.exp(logits - row_max))
    row_total = jnp.sum(weights, axis=1, keepdims=True)
    log_total = row_max[:, 0] + jnp.log(row_total[:, 0])
    mean_loss = jnp.mean(log_total - jnp.sum(jnp.where(onehot, logits, 0.0), axis=1))
    logit_grad = (weights / row_total - onehot.astype(jnp.float32)).astype(jnp.bfloat16)
    own_users = lax.dynamic_slice_in_dim(logit_grad, me * users_here, users_here, axis=0)
    user_grad = jnp.dot(own_users, emb_all, preferred_element_type=jnp.float32).astype(
        jnp.bfloat16
    )
    own_items = lax.dynamic_slice_in_dim(logit_grad, me * items_here, items_here, axis=1)
    emb_grad = contract_rows(own_items, users_all)
    pooled_grad = emb_scale * emb_grad - pooled * emb_scale**3 * jnp.mean(
        pooled * emb_grad, axis=-1, keepdims=True
    )
    normed_grad = jnp.where(inside, pooled_grad[:, None, :] / length_float[:, :, None], 0.0)
    normed_grad = normed_grad.reshape(tok_rows, model_width)
    gain_part = jnp.sum(normed_grad * stream * inverse_root_mean, axis=0)
    scaled = norm_gain * normed_grad
    stream_grad = inverse_root_mean * scaled - stream * inverse_root_mean**3 * jnp.mean(
        scaled * stream, axis=-1, keepdims=True
    )
    residual_grad = stream_grad.astype(jnp.bfloat16)
    weight_grad, gain_all, context_grad = reduce_weight(
        groups, ring, context, residual_grad, weight_all, gain_part[None, :]
    )
    gain_grad = jnp.sum(gain_all[:, 0, :], axis=0)
    return (mean_loss, residual_grad, context_grad, weight_grad, gain_grad, user_grad)


def solution(mesh):
    placed = (
        P(("dp", "fsdp"), None),
        P(("dp", "fsdp"), None),
        P("fsdp", None),
        P(),
        P(("dp", "fsdp"), None),
        P(("dp", "fsdp")),
        P(("dp", "fsdp")),
        P(("dp", "fsdp")),
        P(("dp", "fsdp")),
    )
    return jax.shard_map(
        functools.partial(on_device, mesh.shape["dp"], mesh.shape["fsdp"]),
        mesh=mesh,
        in_specs=placed,
        out_specs=(
            P(),
            P(("dp", "fsdp"), None),
            P(("dp", "fsdp"), None),
            P("fsdp", None),
            P(),
            P(("dp", "fsdp"), None),
        ),
        check_vma=False,
    )
```

```python
import functools

import jax
import jax.numpy as jnp
from jax import lax
from jax.experimental import pallas as pl
from jax.experimental.pallas import tpu as pltpu
from jax.sharding import PartitionSpec as P

EPSILON = 1e-06
MASKED_FILL = -1e30
MESH = pl.DeviceIdType.MESH
CHUNKS = 4


def contract_rows(left, right):
    return lax.dot_general(
        left, right, (((0,), (0,)), ((), ())), preferred_element_type=jnp.float32
    )


def contract_last(left, right):
    return lax.dot_general(
        left, right, (((1,), (1,)), ((), ())), preferred_element_type=jnp.float32
    )


def ring_place(index, count):
    return jnp.where(index % 2 == 0, index // 2, count - 1 - index // 2)


def ring_index(place, count):
    return jnp.where(place < count // 2, 2 * place, 2 * (count - 1 - place) + 1)


def greet(devices):
    barrier = pltpu.get_barrier_semaphore()
    for device in devices:
        pl.semaphore_signal(barrier, inc=1, device_id=device, device_id_type=MESH)
    pl.semaphore_wait(barrier, len(devices))


def greet_all(groups, ring, me):
    total = groups * ring
    barrier = pltpu.get_barrier_semaphore()

    def signal(k, carry):
        peer = lax.rem(me + k, total)
        pl.semaphore_signal(
            barrier, inc=1, device_id=(peer // ring, lax.rem(peer, ring)), device_id_type=MESH
        )
        return carry

    lax.fori_loop(1, total, signal, 0)
    pl.semaphore_wait(barrier, total - 1)


def remote(src, dst, send_sem, recv_sem, device):
    return pltpu.make_async_remote_copy(
        src_ref=src,
        dst_ref=dst,
        send_sem=send_sem,
        recv_sem=recv_sem,
        device_id=device,
        device_id_type=MESH,
    )


def gather_kernel(
    groups, ring, w_in, u_in, k_in, w_out, u_out, k_out,
    own_sem, w_send, w_recv, p_send, p_recv, y_send, y_recv,
    u_send, u_recv, k_send, k_recv, ul_send, ul_recv, kl_send, kl_recv,
    up_send, up_recv, kp_send, kp_recv,
):
    group, index = lax.axis_index("dp"), lax.axis_index("fsdp")
    lines = groups // 2
    split = lines == 2
    slots = CHUNKS - 1 if split else CHUNKS
    line = group // 2
    core = lax.rem(group, 2)
    partner = group + 1 - 2 * core
    across = lax.rem(group + 2, groups)
    place = ring_place(index, ring)
    ends = (
        ring_index(lax.rem(place + 1, ring), ring),
        ring_index(lax.rem(place + ring - 1, ring), ring),
    )
    rows = w_in.shape[0]
    half = rows // 2
    part = half // CHUNKS
    hops = ring - 1

    def owner(m):
        if m == hops + 2:
            return index
        away = -(m // 2) if m % 2 == 0 else m // 2
        return ring_index(lax.rem(place + ring + away, ring), ring)

    def chunk(j):
        if not split or j < CHUNKS - 2:
            return j
        return CHUNKS - 2 + (line if j == CHUNKS - 2 else 1 - line)

    def w_slice(who, j, side=core):
        start = pl.multiple_of(who * rows + side * half + chunk(j) * part, part)
        return w_out.at[pl.ds(start, part), :]

    greet(
        [(lax.rem(group + k, groups), index) for k in range(1, groups)]
        + [(group, end) for end in ends]
    )
    own = [
        pltpu.make_async_copy(
            w_in, w_out.at[pl.ds(pl.multiple_of(index * rows, rows), rows), :], own_sem.at[0]
        ),
        pltpu.make_async_copy(u_in, u_out.at[group * ring + index], own_sem.at[1]),
        pltpu.make_async_copy(k_in, k_out.at[group * ring + index], own_sem.at[2]),
    ]
    for copy in own:
        copy.start()
    for copy in own:
        copy.wait()

    def w_ring(m, j, shift=0):
        ref = w_slice(owner(m + shift), j)
        return remote(ref, ref, w_send.at[m, j], w_recv.at[m, j], (group, ends[m % 2]))

    def w_part(m, j, side=core):
        ref = w_slice(owner(m + 2), j, side)
        return remote(ref, ref, p_send.at[m, j], p_recv.at[m, j], (partner, index))

    def w_across(m, j):
        ref = w_slice(owner(m + 2), j)
        return remote(ref, ref, y_send.at[m], y_recv.at[m], (across, index))

    small = (
        (u_out, u_send, u_recv, ul_send, ul_recv, up_send, up_recv),
        (k_out, k_send, k_recv, kl_send, kl_recv, kp_send, kp_recv),
    )

    def s_ring(a, m, shift):
        out, send, recv = small[a][:3]
        ref = out.at[group * ring + owner(m + shift)]
        return remote(ref, ref, send.at[m], recv.at[m], (group, ends[m % 2]))

    def s_line(a, s, k):
        out, _, _, send, recv = small[a][:5]
        ref = out.at[group * ring + owner(s + 2)]
        peer = lax.rem(group + 2 * k, groups)
        return remote(ref, ref, send.at[s, k - 1], recv.at[s, k - 1], (peer, index))

    def s_line_in(a, s, k):
        out, _, _, send, recv = small[a][:5]
        source = lax.rem(group + groups - 2 * k, groups)
        ref = out.at[source * ring + owner(s + 2)]
        return remote(ref, ref, send.at[s, k - 1], recv.at[s, k - 1], (source, index))

    def s_part(a, s, k):
        out, send, recv = small[a][0], small[a][5], small[a][6]
        source = lax.rem(group + groups - 2 * k, groups)
        ref = out.at[source * ring + owner(s + 2)]
        return remote(ref, ref, send.at[s, k], recv.at[s, k], (partner, index))

    def s_part_in(a, s, k):
        out, send, recv = small[a][0], small[a][5], small[a][6]
        source = lax.rem(partner + groups - 2 * k, groups)
        ref = out.at[source * ring + owner(s + 2)]
        return remote(ref, ref, send.at[s, k], recv.at[s, k], (partner, index))

    def w_pass(s):
        if split:
            w_across(s, CHUNKS - 1).wait_recv()
            w_part(s, CHUNKS - 1).start()

    def spread(s):
        for a in (0, 1):
            for k in range(1, lines):
                s_line(a, s, k).start()
            s_part(a, s, 0).start()

    def s_pass(s):
        for a in (0, 1):
            for k in range(1, lines):
                s_line_in(a, s, k).wait_recv()
                s_part(a, s, k).start()

    for m in range(min(2, hops)):
        for j in range(slots):
            w_ring(m, j).start()
    for m in range(min(2, hops)):
        for a in (0, 1):
            s_ring(a, m, 0).start()
    spread(hops)
    for m in range(hops):
        more = m + 2 < hops
        for j in range(slots):
            w_ring(m, j, 2).wait_recv()
            if more:
                w_ring(m + 2, j).start()
            if split and j == CHUNKS - 2:
                w_across(m, j).start()
            w_part(m, j).start()
        for a in (0, 1):
            s_ring(a, m, 2).wait_recv()
            if more:
                s_ring(a, m + 2, 0).start()
        spread(m)
        if m == 1:
            s_pass(hops)
        if m >= 2:
            w_pass(m - 2)
            s_pass(m - 2)
    for m in range(hops - 2, hops):
        w_pass(m)
        s_pass(m)
    for m in range(hops):
        for j in range(slots):
            w_ring(m, j).wait_send()
        if split:
            w_across(m, CHUNKS - 2).wait_send()
        for j in range(CHUNKS):
            w_part(m, j).wait_send()
            w_part(m, j, 1 - core).wait_recv()
        for a in (0, 1):
            s_ring(a, m, 0).wait_send()
    for m in range(ring):
        for a in (0, 1):
            for k in range(1, lines):
                s_line(a, m, k).wait_send()
            for k in range(lines):
                s_part(a, m, k).wait_send()
                s_part_in(a, m, k).wait_recv()


def gather_inputs(groups, ring, weight, users, keys):
    total = groups * ring
    lines = groups // 2
    rows, width = weight.shape
    dma = pltpu.SemaphoreType.DMA
    vmem = pl.BlockSpec(memory_space=pltpu.VMEM)
    anywhere = pl.BlockSpec(memory_space=pl.ANY)
    return pl.pallas_call(
        functools.partial(gather_kernel, groups, ring),
        out_shape=(
            jax.ShapeDtypeStruct((ring * rows, width), weight.dtype),
            jax.ShapeDtypeStruct((total,) + users.shape, users.dtype),
            jax.ShapeDtypeStruct((total,) + keys.shape, keys.dtype),
        ),
        in_specs=[anywhere, anywhere, anywhere],
        out_specs=(vmem, vmem, vmem),
        scratch_shapes=[dma((3,))]
        + [dma((ring - 1, CHUNKS))] * 4
        + [dma((ring - 1,))] * 2
        + [dma((ring - 1,))] * 4
        + [dma((ring, max(lines - 1, 1)))] * 4
        + [dma((ring, lines))] * 4,
        compiler_params=pltpu.CompilerParams(
            collective_id=0, has_side_effects=True, vmem_limit_bytes=32 << 20
        ),
        name="gather_inputs",
    )(weight, users, keys)


def share_kernel(groups, ring, x_in, x_out, own_sem, send_sem, recv_sem, wide_send, wide_recv):
    group, index = lax.axis_index("dp"), lax.axis_index("fsdp")
    greet(
        [(group, lax.rem(index + k, ring)) for k in range(1, ring)]
        + [(lax.rem(group + k, groups), index) for k in range(1, groups)]
    )

    def along(k, source):
        return remote(
            x_in, x_out.at[group * ring + source], send_sem.at[k - 1], recv_sem.at[k - 1],
            (group, lax.rem(index + k, ring)),
        )

    def wide(k, source):
        ref = x_out.at[pl.ds(source * ring, ring)]
        return remote(
            ref, ref, wide_send.at[k - 1], wide_recv.at[k - 1], (lax.rem(group + k, groups), index)
        )

    for k in range(1, ring):
        along(k, index).start()
    own = pltpu.make_async_copy(x_in, x_out.at[group * ring + index], own_sem)
    own.start()
    own.wait()
    for k in range(1, ring):
        along(k, lax.rem(index + ring - k, ring)).wait_recv()
    for k in range(1, groups):
        wide(k, group).start()
    for k in range(1, ring):
        along(k, index).wait_send()
    for k in range(1, groups):
        wide(k, group).wait_send()
        wide(k, lax.rem(group + groups - k, groups)).wait_recv()


def share(groups, ring, block):
    total = groups * ring
    dma = pltpu.SemaphoreType.DMA
    vmem = pl.BlockSpec(memory_space=pltpu.VMEM)
    return pl.pallas_call(
        functools.partial(share_kernel, groups, ring),
        out_shape=jax.ShapeDtypeStruct((total,) + block.shape, block.dtype),
        in_specs=[vmem],
        out_specs=vmem,
        scratch_shapes=[dma] + [dma((ring - 1,))] * 2 + [dma((groups - 1,))] * 2,
        compiler_params=pltpu.CompilerParams(collective_id=1, has_side_effects=True),
        name="share",
    )(block)


def reduce_kernel(
    groups, ring, part_in, gain_in, out, gain_out,
    cross, held, arrived, totals, lent, borrowed,
    own_sem, g_send, g_recv, x_send, x_recv, r_send, r_recv, t_send, t_recv, o_send, o_recv,
    y_send, y_recv, f_send, f_recv,
):
    total = groups * ring
    group, index = lax.axis_index("dp"), lax.axis_index("fsdp")
    me = group * ring + index
    core = lax.rem(group, 2)
    partner = group + 1 - 2 * core
    place = ring_place(index, ring)
    ends = (
        ring_index(lax.rem(place + 1, ring), ring),
        ring_index(lax.rem(place + ring - 1, ring), ring),
    )
    hops = ring - 1
    rows = part_in.shape[0] // ring
    half = rows // 2
    piece = half // CHUNKS
    lines = groups // 2
    line = group // 2
    split = lines == 2
    slots = CHUNKS - 1 if split else CHUNKS
    across = lax.rem(group + 2, groups)

    def owner(m):
        if m == hops:
            return index
        away = ring // 2 - m // 2 if m % 2 == 0 else m // 2 - (ring - 1) // 2
        return ring_index(lax.rem(place + ring + away, ring), ring)

    def chunk(j):
        if not split or j < CHUNKS - 2:
            return j
        return CHUNKS - 2 + (line if j == CHUNKS - 2 else 1 - line)

    greet_all(groups, ring, me)

    def cross_out(m):
        start = pl.multiple_of(owner(m) * rows + (1 - core) * half, half)
        return remote(
            part_in.at[pl.ds(start, half), :], cross.at[m], x_send.at[m], x_recv.at[m],
            (partner, index),
        )

    for m in range(ring):
        cross_out(m).start()

    def gain_push(k):
        peer = lax.rem(me + k, total)
        return remote(
            gain_in, gain_out.at[me], g_send.at[k - 1], g_recv.at[k - 1],
            (peer // ring, lax.rem(peer, ring)),
        )

    def gain_pull(k):
        source = lax.rem(me + total - k, total)
        return remote(
            gain_in, gain_out.at[source], g_send.at[k - 1], g_recv.at[k - 1],
            (source // ring, lax.rem(source, ring)),
        )

    def start_gain(k, carry):
        gain_push(k).start()
        return carry

    lax.fori_loop(1, total, start_gain, 0)
    own = pltpu.make_async_copy(gain_in, gain_out.at[me], own_sem)
    own.start()

    def ring_copy(s, c):
        at = pl.ds(c * piece, piece)
        return remote(
            held.at[s, at, :], arrived.at[s, at, :], r_send.at[s, c], r_recv.at[s, c],
            (group, ends[s % 2]),
        )

    def local_term(s, j):
        offset = chunk(j) * piece
        start = pl.multiple_of(owner(s) * rows + core * half + offset, piece)
        mine = part_in[pl.ds(start, piece), :].astype(jnp.float32)
        return mine + cross[s, pl.ds(pl.multiple_of(offset, piece), piece), :].astype(jnp.float32)

    def lend(s):
        return remote(lent.at[s], borrowed.at[s], y_send.at[s], y_recv.at[s], (across, index))

    def prepare(s):
        cross_out(s).wait_recv()
        if split:
            lent[s] = local_term(s, CHUNKS - 1).astype(lent.dtype)
            lend(s).start()

    def term_of(s, j):
        term = local_term(s, j)
        if split and j == CHUNKS - 2:
            lend(s).wait_recv()
            term = term + borrowed[s].astype(jnp.float32)
        return term

    for m in range(min(2, hops)):
        prepare(m)
    for m in range(hops):
        for j in range(slots):
            at = pl.ds(j * piece, piece)
            if j == max(CHUNKS - 2, 0) and m + 2 < ring:
                prepare(m + 2)
            term = term_of(m, j)
            if m >= 2:
                ring_copy(m - 2, j).wait_recv()
                term = term + arrived[m - 2, at, :].astype(jnp.float32)
            held[m, at, :] = term.astype(held.dtype)
            ring_copy(m, j).start()
    last = hops

    def total_copy(k, j):
        ref = totals.at[line, pl.ds(j * piece, piece), :]
        return remote(
            ref, ref, t_send.at[k - 1, j], t_recv.at[k - 1, j],
            (lax.rem(group + 2 * k, groups), index),
        )

    def total_in(k, j):
        source = lax.rem(group + groups - 2 * k, groups)
        ref = totals.at[source // 2, pl.ds(j * piece, piece), :]
        return remote(ref, ref, t_send.at[k - 1, j], t_recv.at[k - 1, j], (source, index))

    def out_rows(j, side=core):
        return pl.ds(pl.multiple_of(side * half + chunk(j) * piece, piece), piece)

    def out_copy(j, side):
        ref = out.at[out_rows(j, side), :]
        return remote(ref, ref, o_send.at[j], o_recv.at[j], (partner, index))

    def out_across(j):
        ref = out.at[out_rows(j), :]
        return remote(ref, ref, f_send.at[0], f_recv.at[0], (across, index))

    shared = range(CHUNKS - 2) if split else range(CHUNKS)
    for j in range(slots):
        at = pl.ds(j * piece, piece)
        term = term_of(last, j)
        for m in range(max(hops - 2, 0), hops):
            ring_copy(m, j).wait_recv()
            term = term + arrived[m, at, :].astype(jnp.float32)
        value = term.astype(totals.dtype)
        if j in shared:
            totals[line, at, :] = value
            for k in range(1, lines):
                total_copy(k, j).start()
        else:
            out[out_rows(j), :] = value
            out_across(j).start()
            out_copy(j, core).start()

    for j in shared:
        at = pl.ds(j * piece, piece)
        for k in range(1, lines):
            total_in(k, j).wait_recv()
        value = totals[0, at, :].astype(jnp.float32)
        for other in range(1, lines):
            value = value + totals[other, at, :].astype(jnp.float32)
        out[out_rows(j), :] = value.astype(out.dtype)
        out_copy(j, core).start()
    if split:
        out_across(CHUNKS - 1).wait_recv()
        out_copy(CHUNKS - 1, core).start()

    for m in range(ring):
        cross_out(m).wait_send()
        if split:
            lend(m).wait_send()
    for m in range(hops):
        for j in range(slots):
            ring_copy(m, j).wait_send()
    own.wait()

    def finish_gain(k, carry):
        gain_push(k).wait_send()
        gain_pull(k).wait_recv()
        return carry

    lax.fori_loop(1, total, finish_gain, 0)
    for j in shared:
        for k in range(1, lines):
            total_copy(k, j).wait_send()
    for j in range(CHUNKS):
        out_copy(j, core).wait_send()
        out_copy(j, 1 - core).wait_recv()
    if split:
        out_across(CHUNKS - 2).wait_send()


def reduce_weight(groups, ring, partial, gain):
    total = groups * ring
    rows = partial.shape[0] // ring
    half, width = rows // 2, partial.shape[1]
    dma = pltpu.SemaphoreType.DMA
    vmem = pl.BlockSpec(memory_space=pltpu.VMEM)
    return pl.pallas_call(
        functools.partial(reduce_kernel, groups, ring),
        out_shape=(
            jax.ShapeDtypeStruct((rows, width), partial.dtype),
            jax.ShapeDtypeStruct((total,) + gain.shape, gain.dtype),
        ),
        in_specs=[vmem, vmem],
        out_specs=(vmem, vmem),
        scratch_shapes=[
            pltpu.VMEM((ring, half, width), partial.dtype),
            pltpu.VMEM((ring - 1, half, width), partial.dtype),
            pltpu.VMEM((ring - 1, half, width), partial.dtype),
            pltpu.VMEM((groups // 2, half, width), partial.dtype),
            pltpu.VMEM((ring, half // CHUNKS, width), partial.dtype),
            pltpu.VMEM((ring, half // CHUNKS, width), partial.dtype),
            dma,
            dma((total - 1,)),
            dma((total - 1,)),
            dma((ring,)),
            dma((ring,)),
            dma((ring - 1, CHUNKS)),
            dma((ring - 1, CHUNKS)),
            dma((max(groups // 2 - 1, 1), CHUNKS)),
            dma((max(groups // 2 - 1, 1), CHUNKS)),
            dma((CHUNKS,)),
            dma((CHUNKS,)),
            dma((ring,)),
            dma((ring,)),
            dma((1,)),
            dma((1,)),
        ],
        compiler_params=pltpu.CompilerParams(
            collective_id=2, has_side_effects=True, vmem_limit_bytes=40 << 20
        ),
        name="reduce_weight",
    )(partial, gain)


def on_device(
    groups, ring,
    context, residual, out_weight, norm_gain, user_vectors, positive, item_ids, item_counts, lengths
):
    tok_rows, head_width = context.shape
    model_width = residual.shape[1]
    items_here = lengths.shape[0]
    item_length = tok_rows // items_here
    users_here = user_vectors.shape[0]
    devices_all = groups * ring
    keys = jnp.concatenate([positive, item_ids, item_counts])
    lanes = 128 * pl.cdiv(keys.shape[0], 128)
    keys = jnp.broadcast_to(jnp.pad(keys, (0, lanes - keys.shape[0]))[None, :], (8, lanes))
    weight_all, users_all, keys_all = gather_inputs(groups, ring, out_weight, user_vectors, keys)
    users_all = users_all.reshape(devices_all * users_here, model_width)
    positive_all = keys_all[:, 0, :users_here].reshape(-1)
    ids_all = keys_all[:, 0, users_here : users_here + items_here].reshape(-1)
    counts_all = keys_all[:, 0, users_here + items_here : users_here + 2 * items_here].reshape(-1)
    attended = jnp.dot(context, weight_all, preferred_element_type=jnp.float32)
    stream = residual.astype(jnp.float32) + attended
    inverse_root_mean = lax.rsqrt(jnp.mean(stream * stream, axis=-1, keepdims=True) + EPSILON)
    normed = stream * inverse_root_mean * norm_gain
    positions = jnp.arange(item_length, dtype=jnp.int32)
    inside = (positions[None, :] < lengths[:, None])[:, :, None]
    length_float = lengths.astype(jnp.float32)[:, None]
    normed_items = normed.reshape(items_here, item_length, model_width)
    pooled = jnp.sum(jnp.where(inside, normed_items, 0.0), axis=1) / length_float
    emb_scale = lax.rsqrt(jnp.mean(pooled * pooled, axis=-1, keepdims=True) + EPSILON)
    embedding = (pooled * emb_scale).astype(jnp.bfloat16)
    emb_all = share(groups, ring, embedding).reshape(devices_all * items_here, model_width)
    me = lax.axis_index("dp") * ring + lax.axis_index("fsdp")
    items_all = jnp.arange(ids_all.shape[0], dtype=jnp.int32)
    onehot = items_all[None, :] == positive_all[:, None]
    positive_id = jnp.sum(jnp.where(onehot, ids_all[None, :], 0), axis=1)
    excluded = (ids_all[None, :] == positive_id[:, None]) & jnp.logical_not(onehot)
    scores = contract_last(users_all, emb_all)
    log_counts = jnp.log(counts_all.astype(jnp.float32))
    logits = jnp.where(excluded, MASKED_FILL, scores - log_counts[None, :])
    row_max = jnp.max(logits, axis=1, keepdims=True)
    weights = jnp.where(excluded, 0.0, jnp.exp(logits - row_max))
    row_total = jnp.sum(weights, axis=1, keepdims=True)
    log_total = row_max[:, 0] + jnp.log(row_total[:, 0])
    mean_loss = jnp.mean(log_total - jnp.sum(jnp.where(onehot, logits, 0.0), axis=1))
    logit_grad = (weights / row_total - onehot.astype(jnp.float32)).astype(jnp.bfloat16)
    own_users = lax.dynamic_slice_in_dim(logit_grad, me * users_here, users_here, axis=0)
    user_grad = jnp.dot(own_users, emb_all, preferred_element_type=jnp.float32).astype(
        jnp.bfloat16
    )
    own_items = lax.dynamic_slice_in_dim(logit_grad, me * items_here, items_here, axis=1)
    emb_grad = contract_rows(own_items, users_all)
    pooled_grad = emb_scale * emb_grad - pooled * emb_scale**3 * jnp.mean(
        pooled * emb_grad, axis=-1, keepdims=True
    )
    normed_grad = jnp.where(inside, pooled_grad[:, None, :] / length_float[:, :, None], 0.0)
    normed_grad = normed_grad.reshape(tok_rows, model_width)
    gain_part = jnp.sum(normed_grad * stream * inverse_root_mean, axis=0)
    scaled = norm_gain * normed_grad
    stream_grad = inverse_root_mean * scaled - stream * inverse_root_mean**3 * jnp.mean(
        scaled * stream, axis=-1, keepdims=True
    )
    residual_grad = stream_grad.astype(jnp.bfloat16)
    context_grad = contract_last(residual_grad, weight_all).astype(jnp.bfloat16)
    partial = contract_rows(context, residual_grad).astype(jnp.bfloat16)
    weight_grad, gain_all = reduce_weight(groups, ring, partial, gain_part[None, :])
    gain_grad = jnp.sum(gain_all[:, 0, :], axis=0)
    return (mean_loss, residual_grad, context_grad, weight_grad, gain_grad, user_grad)


def solution(mesh):
    placed = (
        P(("dp", "fsdp"), None),
        P(("dp", "fsdp"), None),
        P("fsdp", None),
        P(),
        P(("dp", "fsdp"), None),
        P(("dp", "fsdp")),
        P(("dp", "fsdp")),
        P(("dp", "fsdp")),
        P(("dp", "fsdp")),
    )
    return jax.shard_map(
        functools.partial(on_device, mesh.shape["dp"], mesh.shape["fsdp"]),
        mesh=mesh,
        in_specs=placed,
        out_specs=(
            P(),
            P(("dp", "fsdp"), None),
            P(("dp", "fsdp"), None),
            P("fsdp", None),
            P(),
            P(("dp", "fsdp"), None),
        ),
        check_vma=False,
    )
```
